768 devices in a mesh: ctx: 64 (over x, y, core), head: 12 (over z).
Axes of the slice: x: 4, y: 8, z: 12, core: 2. Of those that a mesh axis runs over, the one named last changes fastest.
Arguments:
- query: bfloat16 [24576, 3072], P('ctx', 'head'), may hold values from -140 to 140
- key: bfloat16 [24576, 3072], P('ctx', 'head'), may hold values from -6 to 6
- value: bfloat16 [24576, 3072], P('ctx', 'head'), may hold values from -6 to 6
- block_mask: int32 [192, 3], P('ctx'), may hold values 0 or 1
- out_weight: bfloat16 [3072, 4096], P('head'), may hold values from -0.109375 to 0.109375
- cotangent: bfloat16 [24576, 4096], P(('ctx', 'head')), may hold values from -6 to 6
Outputs:
- mixed: bfloat16 [24576, 4096], P(('ctx', 'head'))
- grad_query: bfloat16 [24576, 3072], P('ctx', 'head')
- grad_key: bfloat16 [24576, 3072], P('ctx', 'head')
- grad_value: bfloat16 [24576, 3072], P('ctx', 'head')
The draws below stay inside these ranges and needn't reach their ends.
All inputs are finite; a program needn't handle non-finite values. No bound on the sum of `block_mask` on one device may be relied on, other than what follows from the above.
Results may differ from the reference program's by a relative error of at most 0.006.
Values may be sent and summed in bfloat16 or wider, within the bound.
A program may use at most 64 MiB of HBM per device.

```python
import math
import jax
import jax.numpy as jnp
from jax import lax

D = 4096
DH = 128
BLK = 128
TOK_DEV = 384
HEADS = 24
LENGTH = 24576


def pair_draw(key):
    width = HEADS * DH
    query_base = jnp.clip(jax.random.normal(jax.random.fold_in(key, 11), (LENGTH, width), jnp.float32), -6.0, 6.0)
    key_offset = jnp.clip(jax.random.normal(jax.random.fold_in(key, 12), (LENGTH, width), jnp.float32), -6.0, 6.0)
    return (query_base, key_offset)


def draw_query(key, part):
    return pair_draw(key)[0].astype(jnp.bfloat16)


def draw_key(key, part):
    return pair_draw(key)[1].astype(jnp.bfloat16)


def touch_ends(result, rng, low, top_value):
    longest = result.shape.index(max(result.shape))
    spots = []
    for shift in (0, 1):
        where = [jax.random.randint(jax.random.fold_in(rng, axis), (), 0, length) for axis, length in enumerate(result.shape)]
        where[longest] = (where[longest] + shift) % result.shape[longest]
        spots.append(tuple(where))
    return result.at[spots[0]].set(low).at[spots[1]].set(top_value)


def shard_levels(stream_key, dims, split, low, high):
    level = 1.0
    for dim, parts in split:
        heights = jax.random.uniform(jax.random.fold_in(jax.random.fold_in(stream_key, 6), dim), (parts,), jnp.float32, low / len(split), high / len(split))
        level = level * jnp.repeat(jnp.exp(heights), dims[dim] // parts).reshape((-1,) + (1,) * (len(dims) - 1 - dim))
    return level


def centred(key, shape, scale, most, pieces=(), dtype=jnp.bfloat16):
    array = jax.random.normal(key, shape, jnp.float32) * scale
    if len(pieces) > 0:
        array = shard_levels(key, shape, pieces, -0.22, 0.18) * array
    return jnp.clip(array, min=-most, max=most).astype(dtype)


def setup_inputs(seed: int = 0) -> dict:
    key_of = jax.random.split(jax.random.key(seed), 7)
    return {
        "query": draw_query(jax.random.fold_in(key_of[6], 71), 0),
        "key": draw_key(jax.random.fold_in(key_of[6], 71), 0),
        "value": centred(key_of[2], (LENGTH, HEADS * DH), 1.0, 6.0, ((0, 64), (1, 12))),
        "block_mask": touch_ends((jax.random.randint(key_of[3], (LENGTH // BLK, TOK_DEV // BLK), 0, 2) < 1).astype(jnp.int32), jax.random.fold_in(key_of[3], 1), 0, 1),
        "out_weight": centred(key_of[4], (HEADS * DH, D), (HEADS * DH) ** -0.5, 0.109375, ((0, 12),)),
        "cotangent": centred(key_of[5], (LENGTH, D), 1.0, 6.0, ((0, 768),)),
    }


def keep_table(mask, rows):
    blk = rows // mask.shape[0]
    full = jnp.repeat(jnp.repeat(mask, blk, axis=0), blk, axis=1) > 0
    pos = jnp.arange(rows)
    same = pos[:, None] // blk == pos[None, :] // blk
    causal = pos[:, None] >= pos[None, :]
    return (causal & (full | same), causal)

def f32(x):
    return x.astype(jnp.float32)

def shard_work(q3, k3, v3, g3, mask, linear_state, grad_state, scale):
    rows = q3.shape[0]
    keep, causal = keep_table(mask, rows)
    inv_root = 1.0 / math.sqrt(DH)
    raw = jnp.einsum('ihd,jhd->hij', f32(q3), f32(k3))
    s = jnp.where(keep[None], raw * inv_root, -1e+30)
    top = lax.optimization_barrier(jnp.max(s, -1, keepdims=True))
    ex = jnp.exp(s - top)
    probs = (ex / lax.optimization_barrier(jnp.sum(ex, -1, keepdims=True))).astype(jnp.bfloat16)
    soft = jnp.einsum('hij,jhd->ihd', f32(probs), f32(v3))
    inner = jnp.where(causal[None], raw, 0.0).astype(jnp.bfloat16)
    intra = jnp.einsum('hij,jhd->ihd', f32(inner), f32(v3))
    inter = jnp.einsum('ihd,hde->ihe', f32(q3), linear_state, precision=lax.Precision.HIGHEST)
    attn = (soft + scale * (intra + inter)).astype(jnp.bfloat16)
    dprod = jnp.einsum('ihd,jhd->hij', f32(g3), f32(v3))
    delta = lax.optimization_barrier(jnp.sum(f32(g3) * soft, -1)).T
    dscore = (f32(probs) * (dprod - delta[:, :, None]) * inv_root).astype(jnp.bfloat16)
    dinner = jnp.where(causal[None], dprod, 0.0).astype(jnp.bfloat16)
    grad_q = jnp.einsum('hij,jhd->ihd', f32(dscore), f32(k3)) + scale * (jnp.einsum('hij,jhd->ihd', f32(dinner), f32(k3)) + jnp.einsum('ihb,hab->iha', f32(g3), linear_state, precision=lax.Precision.HIGHEST))
    grad_k = jnp.einsum('hij,ihd->jhd', f32(dscore), f32(q3)) + scale * jnp.einsum('hij,ihd->jhd', f32(dinner), f32(q3)) + jnp.einsum('jhb,hab->jha', f32(v3), grad_state, precision=lax.Precision.HIGHEST)
    value_gradient = jnp.einsum('hij,ihd->jhd', f32(probs), f32(g3)) + scale * jnp.einsum('hij,ihd->jhd', f32(inner), f32(g3)) + jnp.einsum('jha,hab->jhb', f32(k3), grad_state, precision=lax.Precision.HIGHEST)
    width = q3.shape[1] * q3.shape[2]
    return (attn.reshape(rows, width), grad_q.astype(jnp.bfloat16).reshape(rows, width), grad_k.astype(jnp.bfloat16).reshape(rows, width), value_gradient.astype(jnp.bfloat16).reshape(rows, width))

def reference(query, key, value, block_mask, out_weight, cotangent):
    total_rows = query.shape[0]
    rows = TOK_DEV
    shards = total_rows // rows
    heads = query.shape[1] // DH
    scale = 1.0 / math.sqrt(DH * total_rows)
    grad_attn = jnp.dot(cotangent, out_weight.T, preferred_element_type=jnp.float32).astype(jnp.bfloat16)

    def shaped(x):
        return x.reshape(shards, rows, heads, DH)
    qs, ks, vs, gs = (shaped(query), shaped(key), shaped(value), shaped(grad_attn))
    masks = block_mask.reshape(shards, rows // BLK, rows // BLK)
    own = lax.map(lambda a: jnp.einsum('jhd,jhe->hde', f32(a[0]), f32(a[1])), (ks, vs))
    own_grad = lax.map(lambda a: scale * jnp.einsum('ihd,ihe->hde', f32(a[0]), f32(a[1])), (qs, gs))
    zero = jnp.zeros_like(own[:1])
    prefix = jnp.concatenate([zero, jnp.cumsum(own, 0)[:-1]], 0)
    trailing_part = jnp.concatenate([jnp.cumsum(own_grad[::-1], 0)[::-1][1:], zero], 0)
    attn, grad_q, grad_k, value_gradient = lax.map(lambda a: shard_work(a[0], a[1], a[2], a[3], a[4], a[5], a[6], scale), (qs, ks, vs, gs, masks, prefix, trailing_part))
    width = heads * DH
    attn = attn.reshape(total_rows, width)
    mixed = jnp.dot(attn, out_weight, preferred_element_type=jnp.float32).astype(jnp.bfloat16)
    return (mixed, grad_q.reshape(total_rows, width), grad_k.reshape(total_rows, width), value_gradient.reshape(total_rows, width))
```

```python
import functools
import math

import jax
import jax.numpy as jnp
from jax import lax
from jax.experimental import pallas as pl
from jax.experimental.pallas import tpu as pltpu
from jax.sharding import PartitionSpec as P

DH = 128
GROUP = 16
MESH = pl.DeviceIdType.MESH
F32 = jnp.float32
BF16 = jnp.bfloat16


def nn(a, b):
    return lax.dot_general(a, b, (((1,), (0,)), ((), ())), preferred_element_type=F32)


def nt(a, b):
    return lax.dot_general(a, b, (((1,), (1,)), ((), ())), preferred_element_type=F32)


def tn(a, b):
    return lax.dot_general(a, b, (((0,), (0,)), ((), ())), preferred_element_type=F32)


def two(x):
    high = x.astype(BF16)
    return high, (x - high.astype(F32)).astype(BF16)


class Scan:
    def __init__(self, sizes, reverse, part, heard, sums, total, others, result, sems):
        self.group, self.groups = sizes
        self.reverse = reverse
        self.part, self.heard, self.sums = part, heard, sums
        self.total, self.others, self.result = total, others, result
        self.send1, self.recv1, self.send2, self.recv2, self.send3, self.recv3 = sems
        ctx = lax.axis_index("ctx")
        self.r = lax.rem(ctx, self.group)
        self.x = lax.div(ctx, self.group)

    def peer(self, k):
        return lax.rem(self.r + k, self.group)

    def origin(self, k):
        return lax.rem(self.r + self.group - k, self.group)

    def copy1(self, k):
        j = self.peer(k)
        return pltpu.make_async_remote_copy(
            self.part.at[j], self.heard.at[self.r], self.send1.at[k], self.recv1.at[k],
            device_id={"ctx": self.x * self.group + j}, device_id_type=MESH,
        )

    def copy2(self, k):
        j = lax.rem(self.x + k, self.groups)
        return pltpu.make_async_remote_copy(
            self.total, self.others.at[self.x], self.send2.at[k], self.recv2.at[k],
            device_id={"ctx": j * self.group + self.r}, device_id_type=MESH,
        )

    def copy3(self, k):
        j = self.peer(k)
        return pltpu.make_async_remote_copy(
            self.sums.at[j], self.result.at[self.r], self.send3.at[k], self.recv3.at[k],
            device_id={"ctx": self.x * self.group + j}, device_id_type=MESH,
        )

    def each(self, first, last, what):
        def one(k, carry):
            what(k)
            return carry

        lax.fori_loop(first, last, one, 0)

    def start(self):
        self.each(1, self.group, lambda k: self.copy1(k).start())
        self.heard[self.r] = self.part[self.r]

    def middle(self):
        self.each(1, self.group, lambda k: self.copy1(k).wait_recv())
        order = range(self.group)
        acc = jnp.zeros(self.total.shape, F32)
        for p in reversed(order) if self.reverse else order:
            self.sums[p] = acc
            acc = acc + self.heard[p]
        self.total[...] = acc
        self.each(1, self.groups, lambda k: self.copy2(k).start())

    def back(self):
        self.each(1, self.groups, lambda k: self.copy2(k).wait_recv())
        base = jnp.zeros(self.total.shape, F32)
        for k in range(1, self.groups):
            j = lax.rem(self.x + self.groups - k, self.groups)
            before = j > self.x if self.reverse else j < self.x
            base = base + jnp.where(before, self.others[j], 0.0)
        for p in range(self.group):
            self.sums[p] = self.sums[p] + base
        self.each(1, self.group, lambda k: self.copy3(k).start())
        self.result[self.r] = self.sums[self.r]

    def finish(self):
        self.each(1, self.group, lambda k: self.copy3(k).wait_recv())

    def drain(self):
        self.each(1, self.group, lambda k: self.copy1(k).wait_send())
        self.each(1, self.groups, lambda k: self.copy2(k).wait_send())
        self.each(1, self.group, lambda k: self.copy3(k).wait_send())


def kernel(
    sizes, length,
    q_in, k_in, v_in, mask, w_in, cot_in,
    mixed_out, gq_out, gk_out, gv_out,
    q, k, v, w, cot, probs, inner, soft, intra, attn, part_out, g, dsc, din,
    gk_part, gv_part, gq, gk, gv, mixed, first, arrived,
    part, heard, sums, total, others, state,
    load_sem, store_sem, ag_send, ag_recv, rs_send, rs_recv, s1, r1, s2, r2, s3, r3,
):
    nz, group, groups = sizes
    rows = q_in.shape[0]
    blocks = mask.shape[0]
    blk = rows // blocks
    heads = q_in.shape[1] // DH
    scale = 1.0 / math.sqrt(DH * length)
    inv_root = 1.0 / math.sqrt(DH)
    z = lax.axis_index("head")
    ctx = lax.axis_index("ctx")
    up, down = lax.rem(z + 1, nz), lax.rem(z + nz - 1, nz)

    loads = [
        pltpu.make_async_copy(src, dst, load_sem.at[i])
        for i, (src, dst) in enumerate(
            ((k_in, k), (v_in, v), (q_in, q), (w_in, w), (cot_in, cot.at[z]))
        )
    ]
    for load in loads:
        load.start()

    barrier = pltpu.get_barrier_semaphore()
    r, x = lax.rem(ctx, group), lax.div(ctx, group)
    for neighbour in (up, down):
        pl.semaphore_signal(barrier, inc=1, device_id={"head": neighbour}, device_id_type=MESH)

    def greet(j, carry):
        peer = x * group + lax.rem(r + j, group)
        pl.semaphore_signal(barrier, inc=1, device_id={"ctx": peer}, device_id_type=MESH)
        return carry

    lax.fori_loop(1, group, greet, 0)

    def greet_far(j, carry):
        peer = lax.rem(x + j, groups) * group + r
        pl.semaphore_signal(barrier, inc=1, device_id={"ctx": peer}, device_id_type=MESH)
        return carry

    lax.fori_loop(1, groups, greet_far, 0)
    pl.semaphore_wait(barrier, 2 + group - 1 + groups - 1)

    streams = ((0, 0), (0, 1), (1, 0), (1, 1))
    hops = [nz // 2 if half == way else nz - 1 - nz // 2 for half, way in streams]

    def at(way, distance):
        step = distance if way == 0 else -distance
        return lax.rem(z + step + 2 * nz, nz)

    def ag_copy(t, s):
        half, way = streams[t]
        origin = at(way, -s)
        return pltpu.make_async_remote_copy(
            cot_in.at[half] if s == 0 else cot.at[origin, half],
            cot.at[origin, half],
            ag_send.at[t, s], ag_recv.at[t, s],
            device_id={"head": at(way, 1)}, device_id_type=MESH,
        )

    def ag_arrival(t, s):
        half, way = streams[t]
        here = cot.at[at(way, -s - 1), half]
        return pltpu.make_async_remote_copy(
            here, here, ag_send.at[t, s], ag_recv.at[t, s],
            device_id={"head": at(way, 1)}, device_id_type=MESH,
        )

    def ag_forward(s):
        for t in range(4):
            if s < hops[t]:
                if s > 0:
                    ag_arrival(t, s - 1).wait_recv()
                ag_copy(t, s).start()

    def rs_copy(t, s):
        return pltpu.make_async_remote_copy(
            first.at[t] if s == 0 else arrived.at[t, s - 1],
            arrived.at[t, s],
            rs_send.at[t, s], rs_recv.at[t, s],
            device_id={"head": at(streams[t][1], 1)}, device_id_type=MESH,
        )

    def rs_forward(s):
        for t in range(4):
            half, way = streams[t]
            if s < hops[t]:
                own = part_out[at(way, hops[t] - s), half]
                if s == 0:
                    first[t] = own.astype(BF16)
                else:
                    rs_copy(t, s - 1).wait_recv()
                    arrived[t, s - 1] = (arrived[t, s - 1].astype(F32) + own).astype(BF16)
                rs_copy(t, s).start()

    def scan(which):
        return Scan(
            (group, groups), which == 1,
            part.at[which], heard.at[which], sums.at[which], total.at[which],
            others.at[which], state.at[which],
            [sem.at[which] for sem in (s1, r1, s2, r2, s3, r3)],
        )

    linear, trailing = scan(0), scan(1)
    per_head = group // heads
    tri = lax.broadcasted_iota(jnp.int32, (blk, blk), 0) >= lax.broadcasted_iota(
        jnp.int32, (blk, blk), 1
    )

    def cols(h):
        return slice(h * DH, (h + 1) * DH)

    def put_part(which, h, value):
        part[which, h * per_head : (h + 1) * per_head] = value.reshape(per_head, -1, DH)

    def get_state(which, h):
        return state[which, h * per_head : (h + 1) * per_head].reshape(DH, DH)

    def causal(x, i, other):
        last = jnp.where(tri, x[:, i * blk :], other)
        return jnp.concatenate([x[:, : i * blk], last], 1) if i else last

    def softmax_part(h):
        for i in range(blocks):
            here, upto = slice(i * blk, (i + 1) * blk), slice(0, (i + 1) * blk)
            raw = nt(q[here, cols(h)], k[upto, cols(h)])
            scores = causal(raw * inv_root, i, -1e30)
            pieces = [
                jnp.where(mask[i, j] > 0, scores[:, j * blk : (j + 1) * blk], -1e30)
                for j in range(i)
            ]
            scores = jnp.concatenate(pieces + [scores[:, i * blk :]], 1)
            expo = jnp.exp(scores - jnp.max(scores, -1, keepdims=True))
            p = (expo / jnp.sum(expo, -1, keepdims=True)).astype(BF16)
            a = causal(raw, i, 0.0).astype(BF16)
            probs[h, here, upto] = p
            inner[h, here, upto] = a
            soft[h, here] = nn(p, v[upto, cols(h)])
            intra[h, here] = nn(a, v[upto, cols(h)])

    def attn_part(h):
        high, low = two(get_state(0, h))
        inter = nn(q[:, cols(h)], high) + nn(q[:, cols(h)], low)
        attn[:, cols(h)] = (soft[h] + scale * (intra[h] + inter)).astype(BF16)

    tile = min(512, w_in.shape[1])
    tiles = w_in.shape[1] // tile

    def project(lo, hi):
        def one(n, carry):
            c = pl.ds(pl.multiple_of(n * tile, tile), tile)
            part_out[:, :, :, c] = nn(attn[...], w[:, c]).reshape(nz, 2, -1, tile)
            return carry

        lax.fori_loop(lo, hi, one, 0)

    def grad_attn_part(i):
        n = nz // blocks
        g[i * blk : (i + 1) * blk] = nt(
            cot[i * n : (i + 1) * n].reshape(blk, w_in.shape[1]), w[...]
        ).astype(BF16)

    def backward_rows(h):
        high, low = two(get_state(0, h))
        for i in range(blocks):
            here, upto = slice(i * blk, (i + 1) * blk), slice(0, (i + 1) * blk)
            gi = g[here, cols(h)]
            dprod = nt(gi, v[upto, cols(h)])
            delta = jnp.sum(gi.astype(F32) * soft[h, here], -1, keepdims=True)
            ds = (probs[h, here, upto].astype(F32) * (dprod - delta) * inv_root).astype(BF16)
            di = causal(dprod, i, 0.0).astype(BF16)
            dsc[h, here, upto] = ds
            din[h, here, upto] = di
            kk = k[upto, cols(h)]
            gq[here, cols(h)] = (
                nn(ds, kk) + scale * (nn(di, kk) + (nt(gi, high) + nt(gi, low)))
            ).astype(BF16)

    def backward_columns(h):
        for j in range(blocks):
            here, below = slice(j * blk, (j + 1) * blk), slice(j * blk, rows)
            qq, gg = q[below, cols(h)], g[below, cols(h)]
            gk_part[here, cols(h)] = tn(dsc[h, below, here], qq) + scale * tn(
                din[h, below, here], qq
            )
            gv_part[here, cols(h)] = tn(probs[h, below, here], gg) + scale * tn(
                inner[h, below, here], gg
            )

    def backward_last(h):
        high, low = two(get_state(1, h))
        vv, kk = v[:, cols(h)], k[:, cols(h)]
        gk[:, cols(h)] = (gk_part[:, cols(h)] + (nt(vv, high) + nt(vv, low))).astype(BF16)
        gv[:, cols(h)] = (gv_part[:, cols(h)] + (nn(kk, high) + nn(kk, low))).astype(BF16)

    def store(i, src, dst):
        return pltpu.make_async_copy(src, dst, store_sem.at[i])

    ag_forward(0)
    loads[0].wait()
    loads[1].wait()
    for h in range(heads):
        put_part(0, h, tn(k[:, cols(h)], v[:, cols(h)]))
    linear.start()
    loads[2].wait()
    softmax_part(0)
    ag_forward(1)
    for h in range(1, heads):
        softmax_part(h)
    linear.middle()
    ag_forward(2)
    linear.back()
    ag_forward(3)
    linear.finish()
    for h in range(heads):
        attn_part(h)
    loads[3].wait()
    project(0, tiles // 2)
    ag_forward(4)
    project(tiles // 2, tiles)
    for s in range(5, max(hops)):
        ag_forward(s)

    rs_forward(0)
    loads[4].wait()
    for t in range(4):
        ag_arrival(t, hops[t] - 1).wait_recv()
    for i in range(blocks):
        grad_attn_part(i)
    rs_forward(1)
    for h in range(heads):
        put_part(1, h, scale * tn(q[:, cols(h)], g[:, cols(h)]))
    trailing.start()
    backward_rows(0)
    rs_forward(2)
    for h in range(1, heads):
        backward_rows(h)
    store(0, gq, gq_out).start()
    trailing.middle()
    rs_forward(3)
    backward_columns(0)
    trailing.back()
    rs_forward(4)
    for h in range(1, heads):
        backward_columns(h)
    trailing.finish()
    for h in range(heads):
        backward_last(h)
    store(1, gk, gk_out).start()
    store(2, gv, gv_out).start()
    for s in range(5, max(hops)):
        rs_forward(s)
    for half in range(2):
        acc = part_out[z, half]
        for t in range(4):
            if streams[t][0] == half:
                rs_copy(t, hops[t] - 1).wait_recv()
                acc = acc + arrived[t, hops[t] - 1].astype(F32)
        mixed[half] = acc.astype(BF16)
    store(3, mixed, mixed_out).start()

    for t in range(4):
        for s in range(hops[t]):
            ag_copy(t, s).wait_send()
            rs_copy(t, s).wait_send()
    linear.drain()
    trailing.drain()
    for i, (src, dst) in enumerate(((gq, gq_out), (gk, gk_out), (gv, gv_out), (mixed, mixed_out))):
        store(i, src, dst).wait()


def on_device(sizes, length, query, key, value, block_mask, out_weight, cotangent):
    nz, group, groups = sizes
    rows, width = query.shape
    heads = width // DH
    dim = out_weight.shape[1]
    sub = rows // nz // 2
    cotangent = cotangent.reshape(2, sub, dim)
    hop = nz // 2
    piece = (heads * DH // group, DH)
    vmem, dma = pltpu.VMEM, pltpu.SemaphoreType.DMA
    any_space = pl.BlockSpec(memory_space=pl.ANY)
    square = (heads, rows, rows)
    outs = pl.pallas_call(
        functools.partial(kernel, sizes, length),
        out_shape=(
            jax.ShapeDtypeStruct((2, sub, dim), BF16),
            jax.ShapeDtypeStruct((rows, width), BF16),
            jax.ShapeDtypeStruct((rows, width), BF16),
            jax.ShapeDtypeStruct((rows, width), BF16),
        ),
        in_specs=[any_space, any_space, any_space, pl.BlockSpec(memory_space=pltpu.SMEM), any_space, any_space],
        out_specs=(any_space,) * 4,
        scratch_shapes=[
            vmem((rows, width), BF16),
            vmem((rows, width), BF16),
            vmem((rows, width), BF16),
            vmem((width, dim), BF16),
            vmem((nz, 2, sub, dim), BF16),
            vmem(square, BF16),
            vmem(square, BF16),
            vmem((heads, rows, DH), F32),
            vmem((heads, rows, DH), F32),
            vmem((rows, width), BF16),
            vmem((nz, 2, sub, dim), F32),
            vmem((rows, width), BF16),
            vmem(square, BF16),
            vmem(square, BF16),
            vmem((rows, width), F32),
            vmem((rows, width), F32),
            vmem((rows, width), BF16),
            vmem((rows, width), BF16),
            vmem((rows, width), BF16),
            vmem((2, sub, dim), BF16),
            vmem((4, sub, dim), BF16),
            vmem((4, hop, sub, dim), BF16),
            vmem((2, group) + piece, F32),
            vmem((2, group) + piece, F32),
            vmem((2, group) + piece, F32),
            vmem((2,) + piece, F32),
            vmem((2, groups) + piece, F32),
            vmem((2, group) + piece, F32),
            dma((5,)),
            dma((4,)),
            dma((4, hop)),
            dma((4, hop)),
            dma((4, hop)),
            dma((4, hop)),
            dma((2, group)),
            dma((2, group)),
            dma((2, groups)),
            dma((2, groups)),
            dma((2, group)),
            dma((2, group)),
        ],
        compiler_params=pltpu.CompilerParams(
            collective_id=0, has_side_effects=True, vmem_limit_bytes=56 << 20
        ),
        name="mixer",
    )(query, key, value, block_mask, out_weight, cotangent)
    return (outs[0].reshape(2 * sub, dim),) + tuple(outs[1:])


def solution(mesh):
    ctx = mesh.shape["ctx"]
    sizes = (mesh.shape["head"], GROUP, ctx // GROUP)

    def step(query, key, value, block_mask, out_weight, cotangent):
        return on_device(
            sizes, query.shape[0] * ctx, query, key, value, block_mask, out_weight, cotangent
        )

    return jax.shard_map(
        step,
        mesh=mesh,
        in_specs=(
            P("ctx", "head"),
            P("ctx", "head"),
            P("ctx", "head"),
            P("ctx", None),
            P("head", None),
            P(("ctx", "head"), None),
        ),
        out_specs=(P(("ctx", "head"), None), P("ctx", "head"), P("ctx", "head"), P("ctx", "head")),
        check_vma=False,
    )
```

```python
import functools
import math

import jax
import jax.numpy as jnp
from jax import lax
from jax.experimental import pallas as pl
from jax.experimental.pallas import tpu as pltpu
from jax.sharding import PartitionSpec as P

DH = 128
GROUP = 16
SHARE = 2
MESH = pl.DeviceIdType.MESH
F32 = jnp.float32
BF16 = jnp.bfloat16


def nn(a, b):
    return lax.dot_general(a, b, (((1,), (0,)), ((), ())), preferred_element_type=F32)


def nt(a, b):
    return lax.dot_general(a, b, (((1,), (1,)), ((), ())), preferred_element_type=F32)


def tn(a, b):
    return lax.dot_general(a, b, (((0,), (0,)), ((), ())), preferred_element_type=F32)


def two(x):
    high = x.astype(BF16)
    return high, (x - high.astype(F32)).astype(BF16)


class Scan:
    def __init__(self, sizes, reverse, part, heard, sums, total, others, result, sems):
        self.group, self.groups = sizes
        self.reverse = reverse
        self.part, self.heard, self.sums = part, heard, sums
        self.total, self.others, self.result = total, others, result
        self.send1, self.recv1, self.send2, self.recv2, self.send3, self.recv3 = sems
        ctx = lax.axis_index("ctx")
        self.r = lax.rem(ctx, self.group)
        self.x = lax.div(ctx, self.group)

    def peer(self, k):
        return lax.rem(self.r + k, self.group)

    def origin(self, k):
        return lax.rem(self.r + self.group - k, self.group)

    def copy1(self, k):
        j = self.peer(k)
        return pltpu.make_async_remote_copy(
            self.part.at[j], self.heard.at[self.r], self.send1.at[k], self.recv1.at[k],
            device_id={"ctx": self.x * self.group + j}, device_id_type=MESH,
        )

    def copy2(self, k):
        j = lax.rem(self.x + k, self.groups)
        return pltpu.make_async_remote_copy(
            self.total, self.others.at[self.x], self.send2.at[k], self.recv2.at[k],
            device_id={"ctx": j * self.group + self.r}, device_id_type=MESH,
        )

    def copy3(self, k):
        j = self.peer(k)
        return pltpu.make_async_remote_copy(
            self.sums.at[j], self.result.at[self.r], self.send3.at[k], self.recv3.at[k],
            device_id={"ctx": self.x * self.group + j}, device_id_type=MESH,
        )

    def each(self, first, last, what):
        def one(k, carry):
            what(k)
            return carry

        lax.fori_loop(first, last, one, 0)

    def start(self):
        self.each(1, self.group, lambda k: self.copy1(k).start())
        self.heard[self.r] = self.part[self.r]

    def middle(self):
        self.each(1, self.group, lambda k: self.copy1(k).wait_recv())
        order = range(self.group)
        acc = jnp.zeros(self.total.shape, F32)
        for p in reversed(order) if self.reverse else order:
            self.sums[p] = acc
            acc = acc + self.heard[p]
        self.total[...] = acc
        self.each(1, self.groups, lambda k: self.copy2(k).start())

    def back(self):
        self.each(1, self.groups, lambda k: self.copy2(k).wait_recv())
        base = jnp.zeros(self.total.shape, F32)
        for k in range(1, self.groups):
            j = lax.rem(self.x + self.groups - k, self.groups)
            before = j > self.x if self.reverse else j < self.x
            base = base + jnp.where(before, self.others[j], 0.0)
        for p in range(self.group):
            self.sums[p] = self.sums[p] + base
        self.each(1, self.group, lambda k: self.copy3(k).start())
        self.result[self.r] = self.sums[self.r]

    def finish(self):
        self.each(1, self.group, lambda k: self.copy3(k).wait_recv())

    def drain(self):
        self.each(1, self.group, lambda k: self.copy1(k).wait_send())
        self.each(1, self.groups, lambda k: self.copy2(k).wait_send())
        self.each(1, self.group, lambda k: self.copy3(k).wait_send())


def kernel(
    sizes, length,
    q_in, k_in, v_in, mask, w_in, cot_in,
    mixed_out, gq_out, gk_out, gv_out,
    q, k, v, w, cot, probs, inner, soft, intra, attn, attn_sent, attn_held, part_out,
    g_sent, g_heard, g_rows, g, dsc, din,
    gk_part, gv_part, gq, gk, gv, mixed, first, arrived,
    part, heard, sums, total, others, state,
    load_sem, store_sem, ag_send, ag_recv, rs_send, rs_recv, s1, r1, s2, r2, s3, r3,
    wz_send, wz_recv, wx_send, wx_recv, wy_send, wy_recv, wc_send, wc_recv,
    vy_send, vy_recv, vx_send, vx_recv, vc_send, vc_recv,
    at_send, at_recv, gt_send, gt_recv,
):
    nz, group, groups, share = sizes
    span = nz // share
    lines = group // 2
    rows, width = q_in.shape
    dim = w_in.shape[-1]
    blocks = mask.shape[0]
    blk = rows // blocks
    heads = width // DH
    scale = 1.0 / math.sqrt(DH * length)
    inv_root = 1.0 / math.sqrt(DH)
    z = lax.axis_index("head")
    ctx = lax.axis_index("ctx")
    r, x = lax.rem(ctx, group), lax.div(ctx, group)
    y, core = lax.div(r, 2), lax.rem(r, 2)

    def along(distance):
        return lax.rem(z + distance + 2 * nz, nz)

    ahead = (span // 2, span - 1 - span // 2)

    loads = [
        pltpu.make_async_copy(src, dst, load_sem.at[i])
        for i, (src, dst) in enumerate(
            ((k_in, k), (v_in, v), (q_in, q), (w_in, w.at[0]))
            + tuple((cot_in.at[half], cot.at[half, ahead[half]]) for half in range(2))
        )
    ]
    for load in loads:
        load.start()

    barrier = pltpu.get_barrier_semaphore()
    for distance in [1, -1] + [n * span for n in range(1, share)]:
        pl.semaphore_signal(
            barrier, inc=1, device_id={"head": along(distance)}, device_id_type=MESH
        )

    def greet(j, carry):
        peer = x * group + lax.rem(r + j, group)
        pl.semaphore_signal(barrier, inc=1, device_id={"ctx": peer}, device_id_type=MESH)
        return carry

    lax.fori_loop(1, group, greet, 0)

    def greet_far(j, carry):
        peer = lax.rem(x + j, groups) * group + r
        pl.semaphore_signal(barrier, inc=1, device_id={"ctx": peer}, device_id_type=MESH)
        return carry

    lax.fori_loop(1, groups, greet_far, 0)
    pl.semaphore_wait(barrier, 2 + share - 1 + group - 1 + groups - 1)

    streams = ((0, 0), (0, 1), (1, 0), (1, 1))
    sign = (1, -1)
    ag_hops = [ahead[half ^ way] for half, way in streams]
    rs_hops = [ahead[1 ^ half ^ way] for half, way in streams]

    def ag_slot(t, s):
        half, way = streams[t]
        return cot.at[half, ahead[half] - sign[way] * s]

    def ag_copy(t, s):
        half, way = streams[t]
        return pltpu.make_async_remote_copy(
            cot_in.at[half] if s == 0 else ag_slot(t, s),
            ag_slot(t, s + 1),
            ag_send.at[t, s], ag_recv.at[t, s],
            device_id={"head": along(sign[way])}, device_id_type=MESH,
        )

    def ag_forward(s):
        for t in range(4):
            if 0 < s <= ag_hops[t]:
                ag_copy(t, s - 1).wait_recv()
            if s < ag_hops[t]:
                ag_copy(t, s).start()

    def rs_copy(t, s):
        return pltpu.make_async_remote_copy(
            first.at[t] if s == 0 else arrived.at[t, s - 1],
            arrived.at[t, s],
            rs_send.at[t, s], rs_recv.at[t, s],
            device_id={"head": along(sign[streams[t][1]])}, device_id_type=MESH,
        )

    def rs_forward(s):
        for t in range(4):
            half, way = streams[t]
            if s < rs_hops[t]:
                own = part_out[half, ahead[half] + sign[way] * (rs_hops[t] - s)]
                if s == 0:
                    first[t] = own.astype(BF16)
                else:
                    rs_copy(t, s - 1).wait_recv()
                    arrived[t, s - 1] = (arrived[t, s - 1].astype(F32) + own).astype(BF16)
                rs_copy(t, s).start()

    shared = pl.ds(1, share - 1)
    wide = dim // 2
    few = lines // groups
    left = pl.ds(pl.multiple_of(x * (wide // groups), wide // groups), wide // groups)
    right = pl.ds(pl.multiple_of(wide + y * (wide // lines), wide // lines), wide // lines)

    def wz_copy(n, side):
        if side:
            at = (core, pl.ds(x * few, few), slice(None), right)
        else:
            at = (core, y, slice(None), left)
        return pltpu.make_async_remote_copy(
            w_in.at[at], w.at[(share - n,) + at], wz_send.at[side, n], wz_recv.at[side, n],
            device_id={"head": along(n * span)}, device_id_type=MESH,
        )

    def wx_copy(n):
        piece = w.at[shared, core, y, :, left]
        return pltpu.make_async_remote_copy(
            piece, piece, wx_send.at[n], wx_recv.at[n],
            device_id={"ctx": lax.rem(x + n, groups) * group + r}, device_id_type=MESH,
        )

    wy_hops = [lines // 2 if half == way else lines - 1 - lines // 2 for half, way in streams]

    def wy_piece(t, s):
        half, way = streams[t]
        from_y = lax.rem(y - sign[way] * s + lines, lines)
        return w.at[shared, core, from_y, :, pl.ds(half * (wide // 2), wide // 2)]

    def wy_copy(t, s):
        to = lax.rem(y + sign[streams[t][1]] + lines, lines)
        return pltpu.make_async_remote_copy(
            wy_piece(t, s), wy_piece(t, s), wy_send.at[t, s], wy_recv.at[t, s],
            device_id={"ctx": x * group + to * 2 + core}, device_id_type=MESH,
        )

    def to_core(piece, send, recv):
        return pltpu.make_async_remote_copy(
            piece, piece, send, recv,
            device_id={"ctx": x * group + y * 2 + 1 - core}, device_id_type=MESH,
        )

    def wc_copy(t, s):
        return to_core(wy_piece(t, s), wc_send.at[t, s], wc_recv.at[t, s])

    def vy_copy(n):
        piece = w.at[shared, core, pl.ds(x * few, few), :, right]
        return pltpu.make_async_remote_copy(
            piece, piece, vy_send.at[n], vy_recv.at[n],
            device_id={"ctx": x * group + lax.rem(y + n, lines) * 2 + core}, device_id_type=MESH,
        )

    def vx_piece(way, s):
        from_x = lax.rem(x - sign[way] * s + groups, groups)
        halved = 2 * s == groups
        columns = pl.ds(wide + way * (wide // 2), wide // 2) if halved else pl.ds(wide, wide)
        return w.at[shared, core, pl.ds(from_x * few, few), :, columns]

    vx_hops = groups // 2

    def vx_copy(way, s):
        from_x = lax.rem(x - sign[way] * s + groups, groups)
        halved = 2 * (s + 1) == groups
        columns = pl.ds(wide + way * (wide // 2), wide // 2) if halved else pl.ds(wide, wide)
        piece = w.at[shared, core, pl.ds(from_x * few, few), :, columns]
        to = lax.rem(x + sign[way] + groups, groups)
        return pltpu.make_async_remote_copy(
            piece, piece, vx_send.at[way, s], vx_recv.at[way, s],
            device_id={"ctx": to * group + r}, device_id_type=MESH,
        )

    def vc_copy(way, s):
        return to_core(vx_piece(way, s), vc_send.at[way, s], vc_recv.at[way, s])

    wc_all = [(0, 0), (2, 0)] + [(t, s + 1) for t in range(4) for s in range(wy_hops[t])]
    vc_all = [(0, 0)] + [(way, s + 1) for way in range(2) for s in range(vx_hops)]

    def w_start():
        for n in range(1, share):
            for side in range(2):
                wz_copy(n, side).start()

    def w_spread():
        for n in range(1, share):
            wz_copy(n, 0).wait_recv()
        for n in range(1, groups):
            wx_copy(n).start()
        for n in range(1, share):
            wz_copy(n, 1).wait_recv()
        for n in range(1, lines):
            vy_copy(n).start()

    def w_forward(s):
        if s == 0:
            for n in range(1, groups):
                wx_copy(n).wait_recv()
        for t in range(4):
            if 0 < s <= wy_hops[t]:
                wy_copy(t, s - 1).wait_recv()
            if s < wy_hops[t]:
                wy_copy(t, s).start()
            if (t, s) in wc_all:
                wc_copy(t, s).start()

    def v_forward(s):
        if s == 0:
            for n in range(1, lines):
                vy_copy(n).wait_recv()
        for way in range(2):
            if 0 < s <= vx_hops:
                vx_copy(way, s - 1).wait_recv()
            if s < vx_hops:
                vx_copy(way, s).start()
            if (way, s) in vc_all:
                vc_copy(way, s).start()

    def w_finish():
        for t, s in wc_all:
            wc_copy(t, s).wait_recv()
        for way, s in vc_all:
            vc_copy(way, s).wait_recv()

    def w_drain():
        for n in range(1, share):
            for side in range(2):
                wz_copy(n, side).wait_send()
        for n in range(1, groups):
            wx_copy(n).wait_send()
        for t in range(4):
            for s in range(wy_hops[t]):
                wy_copy(t, s).wait_send()
        for t, s in wc_all:
            wc_copy(t, s).wait_send()
        for n in range(1, lines):
            vy_copy(n).wait_send()
        for way in range(2):
            for s in range(vx_hops):
                vx_copy(way, s).wait_send()
        for way, s in vc_all:
            vc_copy(way, s).wait_send()

    def token(n, half, i):
        return along(n * span - ahead[half] + i)

    def attn_copy(n):
        return pltpu.make_async_remote_copy(
            attn_sent.at[n], attn_held.at[share - n], at_send.at[n], at_recv.at[n],
            device_id={"head": along(n * span)}, device_id_type=MESH,
        )

    def attn_exchange():
        for n in range(1, share):
            for half in range(2):
                for i in range(span):
                    attn_sent[n, half, i] = attn[token(n, half, i), half]
            attn_copy(n).start()
        for half in range(2):
            for i in range(span):
                attn_held[0, half, i] = attn[token(0, half, i), half]

    def g_copy(n):
        return pltpu.make_async_remote_copy(
            g_sent.at[n], g_heard.at[share - n], gt_send.at[n], gt_recv.at[n],
            device_id={"head": along(n * span)}, device_id_type=MESH,
        )

    def grad_attn_part(n):
        value = nt(cot[...].reshape(-1, dim), w[n].reshape(width, dim)).astype(BF16)
        value = value.reshape(2, span, -1, width)
        if n == 0:
            g_heard[0] = value
        else:
            g_sent[n] = value
            g_copy(n).start()

    def g_collect():
        for n in range(1, share):
            g_copy(n).wait_recv()
        for n in range(share):
            for half in range(2):
                for i in range(span):
                    g_rows[token(n, half, i), half] = g_heard[n, half, i]
        g[...] = g_rows[...].reshape(rows, width)

    def scan(which):
        return Scan(
            (group, groups), which == 1,
            part.at[which], heard.at[which], sums.at[which], total.at[which],
            others.at[which], state.at[which],
            [sem.at[which] for sem in (s1, r1, s2, r2, s3, r3)],
        )

    linear, trailing = scan(0), scan(1)
    per_head = group // heads
    tri = lax.broadcasted_iota(jnp.int32, (blk, blk), 0) >= lax.broadcasted_iota(
        jnp.int32, (blk, blk), 1
    )

    def cols(h):
        return slice(h * DH, (h + 1) * DH)

    def put_part(which, h, value):
        part[which, h * per_head : (h + 1) * per_head] = value.reshape(per_head, -1, DH)

    def get_state(which, h):
        return state[which, h * per_head : (h + 1) * per_head].reshape(DH, DH)

    def causal(x, i, other):
        last = jnp.where(tri, x[:, i * blk :], other)
        return jnp.concatenate([x[:, : i * blk], last], 1) if i else last

    def softmax_part(h):
        for i in range(blocks):
            here, upto = slice(i * blk, (i + 1) * blk), slice(0, (i + 1) * blk)
            raw = nt(q[here, cols(h)], k[upto, cols(h)])
            scores = causal(raw * inv_root, i, -1e30)
            pieces = [
                jnp.where(mask[i, j] > 0, scores[:, j * blk : (j + 1) * blk], -1e30)
                for j in range(i)
            ]
            scores = jnp.concatenate(pieces + [scores[:, i * blk :]], 1)
            expo = jnp.exp(scores - jnp.max(scores, -1, keepdims=True))
            p = (expo / jnp.sum(expo, -1, keepdims=True)).astype(BF16)
            a = causal(raw, i, 0.0).astype(BF16)
            probs[h, here, upto] = p
            inner[h, here, upto] = a
            soft[h, here] = nn(p, v[upto, cols(h)])
            intra[h, here] = nn(a, v[upto, cols(h)])

    def attn_part(h):
        high, low = two(get_state(0, h))
        inter = nn(q[:, cols(h)], high) + nn(q[:, cols(h)], low)
        value = (soft[h] + scale * (intra[h] + inter)).astype(BF16)
        attn[:, :, :, cols(h)] = value.reshape(nz, 2, -1, DH)

    tile = min(512, dim)
    tiles = dim // tile

    def project():
        def one(n, carry):
            c = pl.ds(pl.multiple_of(n * tile, tile), tile)
            acc = 0.0
            for n in range(share):
                acc = acc + nn(
                    attn_held[n].reshape(-1, width), w[n, :, :, :, c].reshape(width, tile)
                )
            part_out[:, :, :, c] = acc.reshape(2, span, -1, tile)
            return carry

        lax.fori_loop(0, tiles, one, 0)

    def backward_rows(h):
        high, low = two(get_state(0, h))
        for i in range(blocks):
            here, upto = slice(i * blk, (i + 1) * blk), slice(0, (i + 1) * blk)
            gi = g[here, cols(h)]
            dprod = nt(gi, v[upto, cols(h)])
            delta = jnp.sum(gi.astype(F32) * soft[h, here], -1, keepdims=True)
            ds = (probs[h, here, upto].astype(F32) * (dprod - delta) * inv_root).astype(BF16)
            di = causal(dprod, i, 0.0).astype(BF16)
            dsc[h, here, upto] = ds
            din[h, here, upto] = di
            kk = k[upto, cols(h)]
            gq[here, cols(h)] = (
                nn(ds, kk) + scale * (nn(di, kk) + (nt(gi, high) + nt(gi, low)))
            ).astype(BF16)

    def backward_columns(h):
        for j in range(blocks):
            here, below = slice(j * blk, (j + 1) * blk), slice(j * blk, rows)
            qq, gg = q[below, cols(h)], g[below, cols(h)]
            gk_part[here, cols(h)] = tn(dsc[h, below, here], qq) + scale * tn(
                din[h, below, here], qq
            )
            gv_part[here, cols(h)] = tn(probs[h, below, here], gg) + scale * tn(
                inner[h, below, here], gg
            )

    def backward_last(h):
        high, low = two(get_state(1, h))
        vv, kk = v[:, cols(h)], k[:, cols(h)]
        gk[:, cols(h)] = (gk_part[:, cols(h)] + (nt(vv, high) + nt(vv, low))).astype(BF16)
        gv[:, cols(h)] = (gv_part[:, cols(h)] + (nn(kk, high) + nn(kk, low))).astype(BF16)

    def store(i, src, dst):
        return pltpu.make_async_copy(src, dst, store_sem.at[i])

    w_start()
    ag_forward(0)
    loads[0].wait()
    loads[1].wait()
    for h in range(heads):
        put_part(0, h, tn(k[:, cols(h)], v[:, cols(h)]))
    linear.start()
    loads[2].wait()
    w_spread()
    softmax_part(0)
    ag_forward(1)
    linear.middle()
    w_forward(0)
    v_forward(0)
    for h in range(1, heads):
        softmax_part(h)
    w_forward(1)
    linear.back()
    ag_forward(2)
    w_forward(2)
    v_forward(1)
    w_forward(3)
    ag_forward(3)
    linear.finish()
    for h in range(heads):
        attn_part(h)
    attn_exchange()
    v_forward(2)
    for s in range(4, max(wy_hops) + 1):
        w_forward(s)
    for s in range(4, max(ag_hops) + 1):
        ag_forward(s)
    w_finish()

    for load in loads[3:]:
        load.wait()
    for n in reversed(range(share)):
        grad_attn_part(n)
    for n in range(1, share):
        attn_copy(n).wait_recv()
    project()
    rs_forward(0)
    g_collect()
    for h in range(heads):
        put_part(1, h, scale * tn(q[:, cols(h)], g[:, cols(h)]))
    trailing.start()
    backward_rows(0)
    rs_forward(1)
    for h in range(1, heads):
        backward_rows(h)
    store(0, gq, gq_out).start()
    trailing.middle()
    rs_forward(2)
    backward_columns(0)
    trailing.back()
    rs_forward(3)
    for h in range(1, heads):
        backward_columns(h)
    trailing.finish()
    for h in range(heads):
        backward_last(h)
    store(1, gk, gk_out).start()
    store(2, gv, gv_out).start()
    for s in range(4, max(rs_hops)):
        rs_forward(s)
    for half in range(2):
        acc = part_out[half, ahead[half]]
        for t in range(4):
            if streams[t][0] == half and rs_hops[t]:
                rs_copy(t, rs_hops[t] - 1).wait_recv()
                acc = acc + arrived[t, rs_hops[t] - 1].astype(F32)
        mixed[half] = acc.astype(BF16)
    store(3, mixed, mixed_out).start()

    for t in range(4):
        for s in range(ag_hops[t]):
            ag_copy(t, s).wait_send()
        for s in range(rs_hops[t]):
            rs_copy(t, s).wait_send()
    linear.drain()
    trailing.drain()
    w_drain()
    for n in range(1, share):
        attn_copy(n).wait_send()
        g_copy(n).wait_send()
    for i, (src, dst) in enumerate(((gq, gq_out), (gk, gk_out), (gv, gv_out), (mixed, mixed_out))):
        store(i, src, dst).wait()


def publish(*refs):
    sem = refs[-1]
    half = len(refs) // 2
    copies = [pltpu.make_async_copy(refs[i], refs[half + i], sem.at[i]) for i in range(half)]
    for copy in copies:
        copy.start()
    for copy in copies:
        copy.wait()


def on_device(sizes, length, query, key, value, block_mask, out_weight, cotangent):
    nz, group, groups, share = sizes
    rows, width = query.shape
    heads = width // DH
    dim = out_weight.shape[1]
    sub = rows // nz // 2
    span = nz // share
    hop = max(span // 2, 1)
    lines = group // 2
    cotangent = cotangent.reshape(2, sub, dim)
    out_weight = out_weight.reshape(2, lines, width // group, dim)
    piece = (heads * DH // group, DH)
    vmem, dma = pltpu.VMEM, pltpu.SemaphoreType.DMA
    any_space = pl.BlockSpec(memory_space=pl.ANY)
    square = (heads, rows, rows)
    rows_of = (2, span, sub)
    shapes = (
        jax.ShapeDtypeStruct((2, sub, dim), BF16),
        jax.ShapeDtypeStruct((rows, width), BF16),
        jax.ShapeDtypeStruct((rows, width), BF16),
        jax.ShapeDtypeStruct((rows, width), BF16),
    )
    outs = pl.pallas_call(
        functools.partial(kernel, sizes, length),
        out_shape=shapes,
        in_specs=[any_space] * 3 + [pl.BlockSpec(memory_space=pltpu.SMEM)] + [any_space] * 2,
        out_specs=(any_space,) * 4,
        scratch_shapes=[
            vmem((rows, width), BF16),
            vmem((rows, width), BF16),
            vmem((rows, width), BF16),
            vmem((share,) + out_weight.shape, BF16),
            vmem(rows_of + (dim,), BF16),
            vmem(square, BF16),
            vmem(square, BF16),
            vmem((heads, rows, DH), F32),
            vmem((heads, rows, DH), F32),
            vmem((nz, 2, sub, width), BF16),
            vmem((share,) + rows_of + (width,), BF16),
            vmem((share,) + rows_of + (width,), BF16),
            vmem(rows_of + (dim,), F32),
            vmem((share,) + rows_of + (width,), BF16),
            vmem((share,) + rows_of + (width,), BF16),
            vmem((nz, 2, sub, width), BF16),
            vmem((rows, width), BF16),
            vmem(square, BF16),
            vmem(square, BF16),
            vmem((rows, width), F32),
            vmem((rows, width), F32),
            vmem((rows, width), BF16),
            vmem((rows, width), BF16),
            vmem((rows, width), BF16),
            vmem((2, sub, dim), BF16),
            vmem((4, sub, dim), BF16),
            vmem((4, hop, sub, dim), BF16),
            vmem((2, group) + piece, F32),
            vmem((2, group) + piece, F32),
            vmem((2, group) + piece, F32),
            vmem((2,) + piece, F32),
            vmem((2, groups) + piece, F32),
            vmem((2, group) + piece, F32),
            dma((6,)),
            dma((4,)),
        ]
        + [dma((4, hop))] * 4
        + [dma((2, group))] * 2
        + [dma((2, groups))] * 2
        + [dma((2, group))] * 2
        + [dma((2, share))] * 2
        + [dma((groups,))] * 2
        + [dma((4, lines // 2))] * 2
        + [dma((4, lines // 2 + 1))] * 2
        + [dma((lines,))] * 2
        + [dma((2, groups // 2))] * 2
        + [dma((2, groups // 2 + 1))] * 2
        + [dma((share,))] * 4,
        compiler_params=pltpu.CompilerParams(
            collective_id=0, has_side_effects=True, vmem_limit_bytes=56 << 20
        ),
        name="mixer",
    )(query, key, value, block_mask, out_weight, cotangent)
    outs = pl.pallas_call(
        publish,
        out_shape=shapes,
        in_specs=[pl.BlockSpec(memory_space=pltpu.VMEM)] * 4,
        out_specs=(any_space,) * 4,
        scratch_shapes=[dma((4,))],
        name="publish",
    )(*outs)
    return (outs[0].reshape(2 * sub, dim),) + tuple(outs[1:])


def solution(mesh):
    ctx = mesh.shape["ctx"]
    sizes = (mesh.shape["head"], GROUP, ctx // GROUP, SHARE)

    def step(query, key, value, block_mask, out_weight, cotangent):
        return on_device(
            sizes, query.shape[0] * ctx, query, key, value, block_mask, out_weight, cotangent
        )

    return jax.shard_map(
        step,
        mesh=mesh,
        in_specs=(
            P("ctx", "head"),
            P("ctx", "head"),
            P("ctx", "head"),
            P("ctx", None),
            P("head", None),
            P(("ctx", "head"), None),
        ),
        out_specs=(P(("ctx", "head"), None), P("ctx", "head"), P("ctx", "head"), P("ctx", "head")),
        check_vma=False,
    )
```

```python
import functools
import math

import jax
import jax.numpy as jnp
from jax import lax
from jax.experimental import pallas as pl
from jax.experimental.pallas import tpu as pltpu
from jax.sharding import PartitionSpec as P

DH = 128
GROUP = 16
SHARE = 2
MESH = pl.DeviceIdType.MESH
F32 = jnp.float32
BF16 = jnp.bfloat16


def nn(a, b):
    return lax.dot_general(a, b, (((1,), (0,)), ((), ())), preferred_element_type=F32)


def nt(a, b):
    return lax.dot_general(a, b, (((1,), (1,)), ((), ())), preferred_element_type=F32)


def tn(a, b):
    return lax.dot_general(a, b, (((0,), (0,)), ((), ())), preferred_element_type=F32)


class Scan:
    def __init__(self, sizes, reverse, part, heard, sums, back, total, others, result, sems):
        self.group, self.groups = sizes
        self.reverse = reverse
        self.part, self.heard, self.sums, self.outgoing = part, heard, sums, back
        self.total, self.others, self.result = total, others, result
        self.send1, self.recv1, self.send2, self.recv2, self.send3, self.recv3 = sems
        ctx = lax.axis_index("ctx")
        self.r = lax.rem(ctx, self.group)
        self.x = lax.div(ctx, self.group)

    def peer(self, k):
        return lax.rem(self.r + k, self.group)

    def origin(self, k):
        return lax.rem(self.r + self.group - k, self.group)

    def copy1(self, k):
        j = self.peer(k)
        return pltpu.make_async_remote_copy(
            self.part.at[j], self.heard.at[self.r], self.send1.at[k], self.recv1.at[k],
            device_id={"ctx": self.x * self.group + j}, device_id_type=MESH,
        )

    def copy2(self, k):
        j = lax.rem(self.x + k, self.groups)
        return pltpu.make_async_remote_copy(
            self.total, self.others.at[self.x], self.send2.at[k], self.recv2.at[k],
            device_id={"ctx": j * self.group + self.r}, device_id_type=MESH,
        )

    def copy3(self, k):
        j = self.peer(k)
        return pltpu.make_async_remote_copy(
            self.outgoing.at[j], self.result.at[self.r], self.send3.at[k], self.recv3.at[k],
            device_id={"ctx": self.x * self.group + j}, device_id_type=MESH,
        )

    def each(self, first, last, what):
        def one(k, carry):
            what(k)
            return carry

        lax.fori_loop(first, last, one, 0)

    def start(self):
        self.each(1, self.group, lambda k: self.copy1(k).start())
        self.heard[self.r] = self.part[self.r]

    def middle(self):
        self.each(1, self.group, lambda k: self.copy1(k).wait_recv())
        order = range(self.group)
        acc = jnp.zeros(self.total.shape, F32)
        for p in reversed(order) if self.reverse else order:
            self.sums[p] = acc
            acc = acc + self.heard[p]
        self.total[...] = acc
        self.each(1, self.groups, lambda k: self.copy2(k).start())

    def back(self):
        self.each(1, self.groups, lambda k: self.copy2(k).wait_recv())
        base = jnp.zeros(self.total.shape, F32)
        for k in range(1, self.groups):
            j = lax.rem(self.x + self.groups - k, self.groups)
            before = j > self.x if self.reverse else j < self.x
            base = base + jnp.where(before, self.others[j], 0.0)
        for p in range(self.group):
            self.outgoing[p] = (self.sums[p] + base).astype(BF16)
        self.each(1, self.group, lambda k: self.copy3(k).start())
        self.result[self.r] = self.outgoing[self.r]

    def finish(self):
        self.each(1, self.group, lambda k: self.copy3(k).wait_recv())

    def drain(self):
        self.each(1, self.group, lambda k: self.copy1(k).wait_send())
        self.each(1, self.groups, lambda k: self.copy2(k).wait_send())
        self.each(1, self.group, lambda k: self.copy3(k).wait_send())


def kernel(
    sizes, length,
    q_in, k_in, v_in, mask, w_in, cot_in,
    mixed_out, gq_out, gk_out, gv_out,
    q, k, v, w, cot, probs, inner, soft, intra, attn, attn_sent, attn_held, part_out,
    g_sent, g_heard, g_rows, g, dsc, din,
    gk_part, gv_part, gq, gk, gv, mixed, first, arrived,
    part, heard, sums, back, total, others, state,
    load_sem, store_sem, ag_send, ag_recv, rs_send, rs_recv, s1, r1, s2, r2, s3, r3,
    wz_send, wz_recv, wx_send, wx_recv, wy_send, wy_recv, wc_send, wc_recv,
    vy_send, vy_recv, vx_send, vx_recv, vc_send, vc_recv,
    at_send, at_recv, gt_send, gt_recv,
):
    nz, group, groups, share = sizes
    span = nz // share
    lines = group // 2
    rows, width = q_in.shape
    dim = w_in.shape[-1]
    blocks = mask.shape[0]
    blk = rows // blocks
    heads = width // DH
    scale = 1.0 / math.sqrt(DH * length)
    inv_root = 1.0 / math.sqrt(DH)
    z = lax.axis_index("head")
    ctx = lax.axis_index("ctx")
    r, x = lax.rem(ctx, group), lax.div(ctx, group)
    y, core = lax.div(r, 2), lax.rem(r, 2)

    def along(distance):
        return lax.rem(z + distance + 2 * nz, nz)

    ahead = (span // 2, span - 1 - span // 2)

    loads = [
        pltpu.make_async_copy(src, dst, load_sem.at[i])
        for i, (src, dst) in enumerate(
            ((k_in, k), (v_in, v), (q_in, q), (w_in, w.at[0]))
            + tuple((cot_in.at[half], cot.at[half, ahead[half]]) for half in range(2))
        )
    ]
    for load in loads:
        load.start()

    barrier = pltpu.get_barrier_semaphore()
    for distance in [1, -1] + [n * span for n in range(1, share)]:
        pl.semaphore_signal(
            barrier, inc=1, device_id={"head": along(distance)}, device_id_type=MESH
        )

    def greet(j, carry):
        peer = x * group + lax.rem(r + j, group)
        pl.semaphore_signal(barrier, inc=1, device_id={"ctx": peer}, device_id_type=MESH)
        return carry

    lax.fori_loop(1, group, greet, 0)

    def greet_far(j, carry):
        peer = lax.rem(x + j, groups) * group + r
        pl.semaphore_signal(barrier, inc=1, device_id={"ctx": peer}, device_id_type=MESH)
        return carry

    lax.fori_loop(1, groups, greet_far, 0)
    pl.semaphore_wait(barrier, 2 + share - 1 + group - 1 + groups - 1)

    flying = {}

    def go(make, *key):
        make(*key).start()
        flying[(make,) + key] = False

    def got(make, *key):
        make(*key).wait_recv()
        flying[(make,) + key] = True

    def land():
        for (make, *key), heard_of in flying.items():
            if not heard_of:
                make(*key).wait_recv()
            make(*key).wait_send()

    streams = ((0, 0), (0, 1), (1, 0), (1, 1))
    sign = (1, -1)
    ag_hops = [ahead[half ^ way] for half, way in streams]
    rs_hops = [ahead[1 ^ half ^ way] for half, way in streams]

    def ag_slot(t, s):
        half, way = streams[t]
        return cot.at[half, ahead[half] - sign[way] * s]

    def ag_copy(t, s):
        half, way = streams[t]
        return pltpu.make_async_remote_copy(
            cot_in.at[half] if s == 0 else ag_slot(t, s),
            ag_slot(t, s + 1),
            ag_send.at[t, s], ag_recv.at[t, s],
            device_id={"head": along(sign[way])}, device_id_type=MESH,
        )

    def ag_forward(s):
        for t in range(4):
            if 0 < s <= ag_hops[t]:
                got(ag_copy, t, s - 1)
            if s < ag_hops[t]:
                go(ag_copy, t, s)

    def rs_copy(t, s):
        return pltpu.make_async_remote_copy(
            first.at[t] if s == 0 else arrived.at[t, s - 1],
            arrived.at[t, s],
            rs_send.at[t, s], rs_recv.at[t, s],
            device_id={"head": along(sign[streams[t][1]])}, device_id_type=MESH,
        )

    def rs_forward(s):
        for t in range(4):
            half, way = streams[t]
            if s < rs_hops[t]:
                own = part_out[half, ahead[half] + sign[way] * (rs_hops[t] - s)]
                if s == 0:
                    first[t] = own.astype(BF16)
                else:
                    got(rs_copy, t, s - 1)
                    arrived[t, s - 1] = (arrived[t, s - 1].astype(F32) + own).astype(BF16)
                go(rs_copy, t, s)

    shared = pl.ds(1, share - 1)
    near = dim * 1 // 4
    wide = dim - near
    few = lines // groups
    left = pl.ds(pl.multiple_of(x * (near // groups), near // groups), near // groups)
    right = pl.ds(pl.multiple_of(near + y * (wide // lines), 128), wide // lines)

    def wz_copy(n, side):
        if side:
            at = (core, pl.ds(x * few, few), slice(None), right)
        else:
            at = (core, y, slice(None), left)
        return pltpu.make_async_remote_copy(
            w_in.at[at], w.at[(share - n,) + at], wz_send.at[side, n], wz_recv.at[side, n],
            device_id={"head": along(n * span)}, device_id_type=MESH,
        )

    def wx_copy(n):
        piece = w.at[shared, core, y, :, left]
        return pltpu.make_async_remote_copy(
            piece, piece, wx_send.at[n], wx_recv.at[n],
            device_id={"ctx": lax.rem(x + n, groups) * group + r}, device_id_type=MESH,
        )

    wy_hops = [lines // 2 if half == way else lines - 1 - lines // 2 for half, way in streams]

    def wy_piece(t, s):
        half, way = streams[t]
        from_y = lax.rem(y - sign[way] * s + lines, lines)
        return w.at[shared, core, from_y, :, pl.ds(half * (near // 2), near // 2)]

    def wy_copy(t, s):
        to = lax.rem(y + sign[streams[t][1]] + lines, lines)
        return pltpu.make_async_remote_copy(
            wy_piece(t, s), wy_piece(t, s), wy_send.at[t, s], wy_recv.at[t, s],
            device_id={"ctx": x * group + to * 2 + core}, device_id_type=MESH,
        )

    def to_core(piece, send, recv):
        return pltpu.make_async_remote_copy(
            piece, piece, send, recv,
            device_id={"ctx": x * group + y * 2 + 1 - core}, device_id_type=MESH,
        )

    def wc_copy(t, s):
        return to_core(wy_piece(t, s), wc_send.at[t, s], wc_recv.at[t, s])

    def vy_copy(n):
        piece = w.at[shared, core, pl.ds(x * few, few), :, right]
        return pltpu.make_async_remote_copy(
            piece, piece, vy_send.at[n], vy_recv.at[n],
            device_id={"ctx": x * group + lax.rem(y + n, lines) * 2 + core}, device_id_type=MESH,
        )

    def vx_piece(way, s):
        from_x = lax.rem(x - sign[way] * s + groups, groups)
        halved = 2 * s == groups
        columns = pl.ds(near + way * (wide // 2), wide // 2) if halved else pl.ds(near, wide)
        return w.at[shared, core, pl.ds(from_x * few, few), :, columns]

    vx_hops = groups // 2

    def vx_copy(way, s):
        from_x = lax.rem(x - sign[way] * s + groups, groups)
        halved = 2 * (s + 1) == groups
        columns = pl.ds(near + way * (wide // 2), wide // 2) if halved else pl.ds(near, wide)
        piece = w.at[shared, core, pl.ds(from_x * few, few), :, columns]
        to = lax.rem(x + sign[way] + groups, groups)
        return pltpu.make_async_remote_copy(
            piece, piece, vx_send.at[way, s], vx_recv.at[way, s],
            device_id={"ctx": to * group + r}, device_id_type=MESH,
        )

    def vc_copy(way, s):
        return to_core(vx_piece(way, s), vc_send.at[way, s], vc_recv.at[way, s])

    wc_all = [(0, 0), (2, 0)] + [(t, s + 1) for t in range(4) for s in range(wy_hops[t])]
    vc_all = [(0, 0)] + [(way, s + 1) for way in range(2) for s in range(vx_hops)]

    def w_start():
        for n in range(1, share):
            for side in range(2):
                go(wz_copy, n, side)

    def w_spread():
        for n in range(1, share):
            got(wz_copy, n, 0)
        for n in range(1, groups):
            go(wx_copy, n)
        for n in range(1, share):
            got(wz_copy, n, 1)
        for n in range(1, lines):
            go(vy_copy, n)

    def w_forward(s):
        if s == 0:
            for n in range(1, groups):
                got(wx_copy, n)
        for t in range(4):
            if 0 < s <= wy_hops[t]:
                got(wy_copy, t, s - 1)
            if s < wy_hops[t]:
                go(wy_copy, t, s)
            if (t, s) in wc_all:
                go(wc_copy, t, s)

    def v_forward(s):
        if s == 0:
            for n in range(1, lines):
                got(vy_copy, n)
        for way in range(2):
            if 0 < s <= vx_hops:
                got(vx_copy, way, s - 1)
            if s < vx_hops:
                go(vx_copy, way, s)
            if (way, s) in vc_all:
                go(vc_copy, way, s)

    def w_finish():
        for t, s in wc_all:
            got(wc_copy, t, s)
        for way, s in vc_all:
            got(vc_copy, way, s)

    def token(n, half, i):
        return along(n * span - ahead[half] + i)

    def attn_copy(n):
        return pltpu.make_async_remote_copy(
            attn_sent.at[n], attn_held.at[share - n], at_send.at[n], at_recv.at[n],
            device_id={"head": along(n * span)}, device_id_type=MESH,
        )

    def attn_exchange():
        for n in range(1, share):
            for half in range(2):
                for i in range(span):
                    attn_sent[n, half, i] = attn[token(n, half, i), half]
            go(attn_copy, n)
        for half in range(2):
            for i in range(span):
                attn_held[0, half, i] = attn[token(0, half, i), half]

    def g_copy(n):
        return pltpu.make_async_remote_copy(
            g_sent.at[n], g_heard.at[share - n], gt_send.at[n], gt_recv.at[n],
            device_id={"head": along(n * span)}, device_id_type=MESH,
        )

    def grad_attn_part(n):
        value = nt(cot[...].reshape(-1, dim), w[n].reshape(width, dim)).astype(BF16)
        value = value.reshape(2, span, -1, width)
        if n == 0:
            g_heard[0] = value
        else:
            g_sent[n] = value
            go(g_copy, n)

    def g_collect():
        for n in range(1, share):
            got(g_copy, n)
        for n in range(share):
            for half in range(2):
                for i in range(span):
                    g_rows[token(n, half, i), half] = g_heard[n, half, i]
        g[...] = g_rows[...].reshape(rows, width)

    def scan(which):
        return Scan(
            (group, groups), which == 1,
            part.at[which], heard.at[which], sums.at[which], back.at[which], total.at[which],
            others.at[which], state.at[which],
            [sem.at[which] for sem in (s1, r1, s2, r2, s3, r3)],
        )

    linear, trailing = scan(0), scan(1)
    per_head = group // heads
    tri = lax.broadcasted_iota(jnp.int32, (blk, blk), 0) >= lax.broadcasted_iota(
        jnp.int32, (blk, blk), 1
    )

    def cols(h):
        return slice(h * DH, (h + 1) * DH)

    def put_part(which, h, value):
        part[which, h * per_head : (h + 1) * per_head] = value.reshape(per_head, -1, DH)

    def get_state(which, h):
        return state[which, h * per_head : (h + 1) * per_head].reshape(DH, DH)

    def causal(x, i, other):
        last = jnp.where(tri, x[:, i * blk :], other)
        return jnp.concatenate([x[:, : i * blk], last], 1) if i else last

    def softmax_part(h):
        for i in range(blocks):
            here, upto = slice(i * blk, (i + 1) * blk), slice(0, (i + 1) * blk)
            raw = nt(q[here, cols(h)], k[upto, cols(h)])
            scores = causal(raw * inv_root, i, -1e30)
            pieces = [
                jnp.where(mask[i, j] > 0, scores[:, j * blk : (j + 1) * blk], -1e30)
                for j in range(i)
            ]
            scores = jnp.concatenate(pieces + [scores[:, i * blk :]], 1)
            expo = jnp.exp(scores - jnp.max(scores, -1, keepdims=True))
            p = (expo / jnp.sum(expo, -1, keepdims=True)).astype(BF16)
            a = causal(raw, i, 0.0).astype(BF16)
            probs[h, here, upto] = p
            inner[h, here, upto] = a
            soft[h, here] = nn(p, v[upto, cols(h)])
            intra[h, here] = nn(a, v[upto, cols(h)])

    def attn_part(h):
        inter = nn(q[:, cols(h)], get_state(0, h))
        value = (soft[h] + scale * (intra[h] + inter)).astype(BF16)
        attn[:, :, :, cols(h)] = value.reshape(nz, 2, -1, DH)

    tile = min(512, dim)
    tiles = dim // tile

    def project():
        def one(n, carry):
            c = pl.ds(pl.multiple_of(n * tile, tile), tile)
            acc = 0.0
            for n in range(share):
                acc = acc + nn(
                    attn_held[n].reshape(-1, width), w[n, :, :, :, c].reshape(width, tile)
                )
            part_out[:, :, :, c] = acc.reshape(2, span, -1, tile)
            return carry

        lax.fori_loop(0, tiles, one, 0)

    def backward_rows(h):
        earlier = get_state(0, h)
        for i in range(blocks):
            here, upto = slice(i * blk, (i + 1) * blk), slice(0, (i + 1) * blk)
            gi = g[here, cols(h)]
            dprod = nt(gi, v[upto, cols(h)])
            delta = jnp.sum(gi.astype(F32) * soft[h, here], -1, keepdims=True)
            ds = (probs[h, here, upto].astype(F32) * (dprod - delta) * inv_root).astype(BF16)
            di = causal(dprod, i, 0.0).astype(BF16)
            dsc[h, here, upto] = ds
            din[h, here, upto] = di
            kk = k[upto, cols(h)]
            gq[here, cols(h)] = (
                nn(ds, kk) + scale * (nn(di, kk) + nt(gi, earlier))
            ).astype(BF16)

    def backward_columns(h):
        for j in range(blocks):
            here, below = slice(j * blk, (j + 1) * blk), slice(j * blk, rows)
            qq, gg = q[below, cols(h)], g[below, cols(h)]
            gk_part[here, cols(h)] = tn(dsc[h, below, here], qq) + scale * tn(
                din[h, below, here], qq
            )
            gv_part[here, cols(h)] = tn(probs[h, below, here], gg) + scale * tn(
                inner[h, below, here], gg
            )

    def backward_last(h):
        later = get_state(1, h)
        vv, kk = v[:, cols(h)], k[:, cols(h)]
        gk[:, cols(h)] = (gk_part[:, cols(h)] + nt(vv, later)).astype(BF16)
        gv[:, cols(h)] = (gv_part[:, cols(h)] + nn(kk, later)).astype(BF16)

    def store(i, src, dst):
        return pltpu.make_async_copy(src, dst, store_sem.at[i])

    def own_state():
        loads[0].wait()
        loads[1].wait()
        for h in range(heads):
            put_part(0, h, tn(k[:, cols(h)], v[:, cols(h)]))

    def own_grad():
        for h in range(heads):
            put_part(1, h, scale * tn(q[:, cols(h)], g[:, cols(h)]))

    def finish_sum():
        for half in range(2):
            acc = part_out[half, ahead[half]]
            for t in range(4):
                if streams[t][0] == half and rs_hops[t]:
                    got(rs_copy, t, rs_hops[t] - 1)
                    acc = acc + arrived[t, rs_hops[t] - 1].astype(F32)
            mixed[half] = acc.astype(BF16)

    results = ((gq, gq_out), (gk, gk_out), (gv, gv_out), (mixed, mixed_out))
    w_start()
    ag_forward(0)
    own_state()
    linear.start()
    loads[2].wait()
    w_spread()
    softmax_part(0)
    ag_forward(1)
    linear.middle()
    w_forward(0)
    v_forward(0)
    softmax_part(1)
    w_forward(1)
    linear.back()
    ag_forward(2)
    w_forward(2)
    v_forward(1)
    w_forward(3)
    ag_forward(3)
    linear.finish()
    for h in range(heads):
        attn_part(h)
    attn_exchange()
    v_forward(2)
    for load in loads[3:]:
        load.wait()
    grad_attn_part(0)
    w_forward(4)
    w_finish()
    grad_attn_part(1)
    got(attn_copy, 1)
    project()
    rs_forward(0)
    g_collect()
    own_grad()
    trailing.start()
    backward_rows(0)
    backward_rows(1)
    store(0, gq, gq_out).start()
    rs_forward(1)
    trailing.middle()
    backward_columns(0)
    backward_columns(1)
    trailing.back()
    rs_forward(2)
    trailing.finish()
    for h in range(heads):
        backward_last(h)
    store(1, gk, gk_out).start()
    store(2, gv, gv_out).start()
    finish_sum()
    store(3, mixed, mixed_out).start()
    land()
    linear.drain()
    trailing.drain()
    for i, (src, dst) in enumerate(results):
        store(i, src, dst).wait()


def publish(*refs):
    sem = refs[-1]
    half = len(refs) // 2
    copies = [pltpu.make_async_copy(refs[i], refs[half + i], sem.at[i]) for i in range(half)]
    for copy in copies:
        copy.start()
    for copy in copies:
        copy.wait()


def on_device(sizes, length, query, key, value, block_mask, out_weight, cotangent):
    nz, group, groups, share = sizes
    rows, width = query.shape
    heads = width // DH
    dim = out_weight.shape[1]
    sub = rows // nz // 2
    span = nz // share
    hop = max(span // 2, 1)
    lines = group // 2
    cotangent = cotangent.reshape(2, sub, dim)
    out_weight = out_weight.reshape(2, lines, width // group, dim)
    piece = (heads * DH // group, DH)
    vmem, dma = pltpu.VMEM, pltpu.SemaphoreType.DMA
    any_space = pl.BlockSpec(memory_space=pl.ANY)
    square = (heads, rows, rows)
    rows_of = (2, span, sub)
    shapes = (
        jax.ShapeDtypeStruct((2, sub, dim), BF16),
        jax.ShapeDtypeStruct((rows, width), BF16),
        jax.ShapeDtypeStruct((rows, width), BF16),
        jax.ShapeDtypeStruct((rows, width), BF16),
    )
    outs = pl.pallas_call(
        functools.partial(kernel, sizes, length),
        out_shape=shapes,
        in_specs=[any_space] * 3 + [pl.BlockSpec(memory_space=pltpu.SMEM)] + [any_space] * 2,
        out_specs=(any_space,) * 4,
        scratch_shapes=[
            vmem((rows, width), BF16),
            vmem((rows, width), BF16),
            vmem((rows, width), BF16),
            vmem((share,) + out_weight.shape, BF16),
            vmem(rows_of + (dim,), BF16),
            vmem(square, BF16),
            vmem(square, BF16),
            vmem((heads, rows, DH), F32),
            vmem((heads, rows, DH), F32),
            vmem((nz, 2, sub, width), BF16),
            vmem((share,) + rows_of + (width,), BF16),
            vmem((share,) + rows_of + (width,), BF16),
            vmem(rows_of + (dim,), F32),
            vmem((share,) + rows_of + (width,), BF16),
            vmem((share,) + rows_of + (width,), BF16),
            vmem((nz, 2, sub, width), BF16),
            vmem((rows, width), BF16),
            vmem(square, BF16),
            vmem(square, BF16),
            vmem((rows, width), F32),
            vmem((rows, width), F32),
            vmem((rows, width), BF16),
            vmem((rows, width), BF16),
            vmem((rows, width), BF16),
            vmem((2, sub, dim), BF16),
            vmem((4, sub, dim), BF16),
            vmem((4, hop, sub, dim), BF16),
            vmem((2, group) + piece, F32),
            vmem((2, group) + piece, F32),
            vmem((2, group) + piece, F32),
            vmem((2, group) + piece, BF16),
            vmem((2,) + piece, F32),
            vmem((2, groups) + piece, F32),
            vmem((2, group) + piece, BF16),
            dma((6,)),
            dma((4,)),
        ]
        + [dma((4, hop))] * 4
        + [dma((2, group))] * 2
        + [dma((2, groups))] * 2
        + [dma((2, group))] * 2
        + [dma((2, share))] * 2
        + [dma((groups,))] * 2
        + [dma((4, lines // 2))] * 2
        + [dma((4, lines // 2 + 1))] * 2
        + [dma((lines,))] * 2
        + [dma((2, groups // 2))] * 2
        + [dma((2, groups // 2 + 1))] * 2
        + [dma((share,))] * 4,
        compiler_params=pltpu.CompilerParams(
            collective_id=0, has_side_effects=True, vmem_limit_bytes=56 << 20
        ),
        name="mixer",
    )(query, key, value, block_mask, out_weight, cotangent)
    outs = pl.pallas_call(
        publish,
        out_shape=shapes,
        in_specs=[pl.BlockSpec(memory_space=pltpu.VMEM)] * 4,
        out_specs=(any_space,) * 4,
        scratch_shapes=[dma((4,))],
        name="publish",
    )(*outs)
    return (outs[0].reshape(2 * sub, dim),) + tuple(outs[1:])


def solution(mesh):
    ctx = mesh.shape["ctx"]
    sizes = (mesh.shape["head"], GROUP, ctx // GROUP, SHARE)

    def step(query, key, value, block_mask, out_weight, cotangent):
        return on_device(
            sizes, query.shape[0] * ctx, query, key, value, block_mask, out_weight, cotangent
        )

    return jax.shard_map(
        step,
        mesh=mesh,
        in_specs=(
            P("ctx", "head"),
            P("ctx", "head"),
            P("ctx", "head"),
            P("ctx", None),
            P("head", None),
            P(("ctx", "head"), None),
        ),
        out_specs=(P(("ctx", "head"), None), P("ctx", "head"), P("ctx", "head"), P("ctx", "head")),
        check_vma=False,
    )
```

```python
import functools
import math

import jax
import jax.numpy as jnp
from jax import lax
from jax.experimental import pallas as pl
from jax.experimental.pallas import tpu as pltpu
from jax.sharding import PartitionSpec as P

DH = 128
GROUP = 16
SHARE = 2
MESH = pl.DeviceIdType.MESH
F32 = jnp.float32
BF16 = jnp.bfloat16


def nn(a, b):
    return lax.dot_general(a, b, (((1,), (0,)), ((), ())), preferred_element_type=F32)


def nt(a, b):
    return lax.dot_general(a, b, (((1,), (1,)), ((), ())), preferred_element_type=F32)


def tn(a, b):
    return lax.dot_general(a, b, (((0,), (0,)), ((), ())), preferred_element_type=F32)


class Scan:
    def __init__(self, sizes, reverse, part, heard, sums, back, total, others, result, sems):
        self.group, self.groups = sizes
        self.reverse = reverse
        self.part, self.heard, self.sums, self.outgoing = part, heard, sums, back
        self.total, self.others, self.result = total, others, result
        self.send1, self.recv1, self.send2, self.recv2, self.send3, self.recv3 = sems
        ctx = lax.axis_index("ctx")
        self.r = lax.rem(ctx, self.group)
        self.x = lax.div(ctx, self.group)

    def peer(self, k):
        return lax.rem(self.r + k, self.group)

    def origin(self, k):
        return lax.rem(self.r + self.group - k, self.group)

    def copy1(self, k):
        j = self.peer(k)
        return pltpu.make_async_remote_copy(
            self.part.at[j], self.heard.at[self.r], self.send1.at[k], self.recv1.at[k],
            device_id={"ctx": self.x * self.group + j}, device_id_type=MESH,
        )

    def copy2(self, k):
        j = lax.rem(self.x + k, self.groups)
        return pltpu.make_async_remote_copy(
            self.total, self.others.at[self.x], self.send2.at[k], self.recv2.at[k],
            device_id={"ctx": j * self.group + self.r}, device_id_type=MESH,
        )

    def copy3(self, k):
        j = self.peer(k)
        return pltpu.make_async_remote_copy(
            self.outgoing.at[j], self.result.at[self.r], self.send3.at[k], self.recv3.at[k],
            device_id={"ctx": self.x * self.group + j}, device_id_type=MESH,
        )

    def each(self, first, last, what):
        def one(k, carry):
            what(k)
            return carry

        lax.fori_loop(first, last, one, 0)

    def start(self):
        self.each(1, self.group, lambda k: self.copy1(k).start())
        self.heard[self.r] = self.part[self.r]

    def middle(self):
        self.each(1, self.group, lambda k: self.copy1(k).wait_recv())
        order = range(self.group)
        acc = jnp.zeros(self.total.shape, F32)
        for p in reversed(order) if self.reverse else order:
            self.sums[p] = acc
            acc = acc + self.heard[p]
        self.total[...] = acc
        self.each(1, self.groups, lambda k: self.copy2(k).start())

    def back(self):
        self.each(1, self.groups, lambda k: self.copy2(k).wait_recv())
        base = jnp.zeros(self.total.shape, F32)
        for k in range(1, self.groups):
            j = lax.rem(self.x + self.groups - k, self.groups)
            before = j > self.x if self.reverse else j < self.x
            base = base + jnp.where(before, self.others[j], 0.0)
        for p in range(self.group):
            self.outgoing[p] = (self.sums[p] + base).astype(BF16)
        self.each(1, self.group, lambda k: self.copy3(k).start())
        self.result[self.r] = self.outgoing[self.r]

    def finish(self):
        self.each(1, self.group, lambda k: self.copy3(k).wait_recv())

    def drain(self):
        self.each(1, self.group, lambda k: self.copy1(k).wait_send())
        self.each(1, self.groups, lambda k: self.copy2(k).wait_send())
        self.each(1, self.group, lambda k: self.copy3(k).wait_send())


def kernel(
    sizes, length,
    q_in, k_in, v_in, mask, w_in, cot_in,
    mixed_out, gq_out, gk_out, gv_out,
    q, k, v, w, cot, probs, inner, soft, intra, attn, attn_sent, attn_held, part_out,
    g_sent, g_heard, g_rows, g, dsc, din,
    gk_part, gv_part, gq, gk, gv, mixed, first, arrived,
    part, heard, sums, back, total, others, state,
    load_sem, store_sem, ag_send, ag_recv, rs_send, rs_recv, s1, r1, s2, r2, s3, r3,
    wz_send, wz_recv,
    vy_send, vy_recv, vx_send, vx_recv, vc_send, vc_recv,
    at_send, at_recv, gt_send, gt_recv,
):
    nz, group, groups, share = sizes
    span = nz // share
    lines = group // 2
    rows, width = q_in.shape
    dim = w_in.shape[-1]
    blocks = mask.shape[0]
    blk = rows // blocks
    heads = width // DH
    scale = 1.0 / math.sqrt(DH * length)
    inv_root = 1.0 / math.sqrt(DH)
    z = lax.axis_index("head")
    ctx = lax.axis_index("ctx")
    r, x = lax.rem(ctx, group), lax.div(ctx, group)
    y, core = lax.div(r, 2), lax.rem(r, 2)

    def along(distance):
        return lax.rem(z + distance + 2 * nz, nz)

    ahead = (span // 2, span - 1 - span // 2)

    loads = [
        pltpu.make_async_copy(src, dst, load_sem.at[i])
        for i, (src, dst) in enumerate(
            ((k_in, k), (v_in, v), (q_in, q), (w_in, w.at[0]))
            + tuple((cot_in.at[half], cot.at[half, ahead[half]]) for half in range(2))
        )
    ]
    for load in loads:
        load.start()

    barrier = pltpu.get_barrier_semaphore()
    for distance in [1, -1] + [n * span for n in range(1, share)]:
        pl.semaphore_signal(
            barrier, inc=1, device_id={"head": along(distance)}, device_id_type=MESH
        )

    def greet(j, carry):
        peer = x * group + lax.rem(r + j, group)
        pl.semaphore_signal(barrier, inc=1, device_id={"ctx": peer}, device_id_type=MESH)
        return carry

    lax.fori_loop(1, group, greet, 0)

    def greet_far(j, carry):
        peer = lax.rem(x + j, groups) * group + r
        pl.semaphore_signal(barrier, inc=1, device_id={"ctx": peer}, device_id_type=MESH)
        return carry

    lax.fori_loop(1, groups, greet_far, 0)
    pl.semaphore_wait(barrier, 2 + share - 1 + group - 1 + groups - 1)

    flying = {}

    def go(make, *key):
        make(*key).start()
        flying[(make,) + key] = False

    def got(make, *key):
        make(*key).wait_recv()
        flying[(make,) + key] = True

    def land():
        for (make, *key), heard_of in flying.items():
            if not heard_of:
                make(*key).wait_recv()
            make(*key).wait_send()

    streams = ((0, 0), (0, 1), (1, 0), (1, 1))
    sign = (1, -1)
    ag_hops = [ahead[half ^ way] for half, way in streams]
    rs_hops = [ahead[1 ^ half ^ way] for half, way in streams]

    def ag_slot(t, s):
        half, way = streams[t]
        return cot.at[half, ahead[half] - sign[way] * s]

    def ag_copy(t, s):
        half, way = streams[t]
        return pltpu.make_async_remote_copy(
            cot_in.at[half] if s == 0 else ag_slot(t, s),
            ag_slot(t, s + 1),
            ag_send.at[t, s], ag_recv.at[t, s],
            device_id={"head": along(sign[way])}, device_id_type=MESH,
        )

    def ag_forward(s):
        for t in range(4):
            if 0 < s <= ag_hops[t]:
                got(ag_copy, t, s - 1)
            if s < ag_hops[t]:
                go(ag_copy, t, s)

    def rs_copy(t, s):
        return pltpu.make_async_remote_copy(
            first.at[t] if s == 0 else arrived.at[t, s - 1],
            arrived.at[t, s],
            rs_send.at[t, s], rs_recv.at[t, s],
            device_id={"head": along(sign[streams[t][1]])}, device_id_type=MESH,
        )

    def rs_forward(s):
        for t in range(4):
            half, way = streams[t]
            if s < rs_hops[t]:
                own = part_out[half, ahead[half] + sign[way] * (rs_hops[t] - s)]
                if s == 0:
                    first[t] = own.astype(BF16)
                else:
                    got(rs_copy, t, s - 1)
                    arrived[t, s - 1] = (arrived[t, s - 1].astype(F32) + own).astype(BF16)
                go(rs_copy, t, s)

    shared = pl.ds(1, share - 1)
    few = lines // groups
    right = pl.ds(pl.multiple_of(y * (dim // lines), dim // lines), dim // lines)

    def wz_copy(n):
        at = (core, pl.ds(x * few, few), slice(None), right)
        return pltpu.make_async_remote_copy(
            w_in.at[at], w.at[(share - n,) + at], wz_send.at[n], wz_recv.at[n],
            device_id={"head": along(n * span)}, device_id_type=MESH,
        )

    def to_core(piece, send, recv):
        return pltpu.make_async_remote_copy(
            piece, piece, send, recv,
            device_id={"ctx": x * group + y * 2 + 1 - core}, device_id_type=MESH,
        )

    def vy_copy(n):
        piece = w.at[shared, core, pl.ds(x * few, few), :, right]
        return pltpu.make_async_remote_copy(
            piece, piece, vy_send.at[n], vy_recv.at[n],
            device_id={"ctx": x * group + lax.rem(y + n, lines) * 2 + core}, device_id_type=MESH,
        )

    def vx_piece(way, s):
        from_x = lax.rem(x - sign[way] * s + groups, groups)
        halved = 2 * s == groups
        columns = pl.ds(way * (dim // 2), dim // 2) if halved else pl.ds(0, dim)
        return w.at[shared, core, pl.ds(from_x * few, few), :, columns]

    vx_hops = groups // 2

    def vx_copy(way, s):
        from_x = lax.rem(x - sign[way] * s + groups, groups)
        halved = 2 * (s + 1) == groups
        columns = pl.ds(way * (dim // 2), dim // 2) if halved else pl.ds(0, dim)
        piece = w.at[shared, core, pl.ds(from_x * few, few), :, columns]
        to = lax.rem(x + sign[way] + groups, groups)
        return pltpu.make_async_remote_copy(
            piece, piece, vx_send.at[way, s], vx_recv.at[way, s],
            device_id={"ctx": to * group + r}, device_id_type=MESH,
        )

    def vc_copy(way, s):
        return to_core(vx_piece(way, s), vc_send.at[way, s], vc_recv.at[way, s])

    vc_all = [(0, 0)] + [(way, s + 1) for way in range(2) for s in range(vx_hops)]

    def w_start():
        for n in range(1, share):
            go(wz_copy, n)

    def w_spread():
        for n in range(1, share):
            got(wz_copy, n)
        for n in range(1, lines):
            go(vy_copy, n)

    def v_forward(s):
        if s == 0:
            for n in range(1, lines):
                got(vy_copy, n)
        for way in range(2):
            if 0 < s <= vx_hops:
                got(vx_copy, way, s - 1)
            if s < vx_hops:
                go(vx_copy, way, s)
            if (way, s) in vc_all:
                go(vc_copy, way, s)

    def w_finish():
        for way, s in vc_all:
            got(vc_copy, way, s)

    def token(n, half, i):
        return along(n * span - ahead[half] + i)

    def attn_copy(n):
        return pltpu.make_async_remote_copy(
            attn_sent.at[n], attn_held.at[share - n], at_send.at[n], at_recv.at[n],
            device_id={"head": along(n * span)}, device_id_type=MESH,
        )

    def attn_exchange():
        for n in range(1, share):
            for half in range(2):
                for i in range(span):
                    attn_sent[n, half, i] = attn[token(n, half, i), half]
            go(attn_copy, n)
        for half in range(2):
            for i in range(span):
                attn_held[0, half, i] = attn[token(0, half, i), half]

    def g_copy(n):
        return pltpu.make_async_remote_copy(
            g_sent.at[n], g_heard.at[share - n], gt_send.at[n], gt_recv.at[n],
            device_id={"head": along(n * span)}, device_id_type=MESH,
        )

    def grad_attn_part(n):
        value = nt(cot[...].reshape(-1, dim), w[n].reshape(width, dim)).astype(BF16)
        value = value.reshape(2, span, -1, width)
        if n == 0:
            g_heard[0] = value
        else:
            g_sent[n] = value
            go(g_copy, n)

    def g_collect():
        for n in range(1, share):
            got(g_copy, n)
        for n in range(share):
            for half in range(2):
                for i in range(span):
                    g_rows[token(n, half, i), half] = g_heard[n, half, i]
        g[...] = g_rows[...].reshape(rows, width)

    def scan(which):
        return Scan(
            (group, groups), which == 1,
            part.at[which], heard.at[which], sums.at[which], back.at[which], total.at[which],
            others.at[which], state.at[which],
            [sem.at[which] for sem in (s1, r1, s2, r2, s3, r3)],
        )

    linear, trailing = scan(0), scan(1)
    per_head = group // heads
    tri = lax.broadcasted_iota(jnp.int32, (blk, blk), 0) >= lax.broadcasted_iota(
        jnp.int32, (blk, blk), 1
    )

    def cols(h):
        return slice(h * DH, (h + 1) * DH)

    def put_part(which, h, value):
        part[which, h * per_head : (h + 1) * per_head] = value.reshape(per_head, -1, DH)

    def get_state(which, h):
        return state[which, h * per_head : (h + 1) * per_head].reshape(DH, DH)

    def causal(x, i, other):
        last = jnp.where(tri, x[:, i * blk :], other)
        return jnp.concatenate([x[:, : i * blk], last], 1) if i else last

    def softmax_part(h):
        for i in range(blocks):
            here, upto = slice(i * blk, (i + 1) * blk), slice(0, (i + 1) * blk)
            raw = nt(q[here, cols(h)], k[upto, cols(h)])
            scores = causal(raw * inv_root, i, -1e30)
            pieces = [
                jnp.where(mask[i, j] > 0, scores[:, j * blk : (j + 1) * blk], -1e30)
                for j in range(i)
            ]
            scores = jnp.concatenate(pieces + [scores[:, i * blk :]], 1)
            expo = jnp.exp(scores - jnp.max(scores, -1, keepdims=True))
            p = (expo / jnp.sum(expo, -1, keepdims=True)).astype(BF16)
            a = causal(raw, i, 0.0).astype(BF16)
            probs[h, here, upto] = p
            inner[h, here, upto] = a
            soft[h, here] = nn(p, v[upto, cols(h)])
            intra[h, here] = nn(a, v[upto, cols(h)])

    def attn_part(h):
        inter = nn(q[:, cols(h)], get_state(0, h))
        value = (soft[h] + scale * (intra[h] + inter)).astype(BF16)
        attn[:, :, :, cols(h)] = value.reshape(nz, 2, -1, DH)

    tile = min(512, dim)
    tiles = dim // tile

    def project():
        def one(n, carry):
            c = pl.ds(pl.multiple_of(n * tile, tile), tile)
            acc = 0.0
            for n in range(share):
                acc = acc + nn(
                    attn_held[n].reshape(-1, width), w[n, :, :, :, c].reshape(width, tile)
                )
            part_out[:, :, :, c] = acc.reshape(2, span, -1, tile)
            return carry

        lax.fori_loop(0, tiles, one, 0)

    def backward_rows(h):
        earlier = get_state(0, h)
        for i in range(blocks):
            here, upto = slice(i * blk, (i + 1) * blk), slice(0, (i + 1) * blk)
            gi = g[here, cols(h)]
            dprod = nt(gi, v[upto, cols(h)])
            delta = jnp.sum(gi.astype(F32) * soft[h, here], -1, keepdims=True)
            ds = (probs[h, here, upto].astype(F32) * (dprod - delta) * inv_root).astype(BF16)
            di = causal(dprod, i, 0.0).astype(BF16)
            dsc[h, here, upto] = ds
            din[h, here, upto] = di
            kk = k[upto, cols(h)]
            gq[here, cols(h)] = (
                nn(ds, kk) + scale * (nn(di, kk) + nt(gi, earlier))
            ).astype(BF16)

    def backward_columns(h):
        for j in range(blocks):
            here, below = slice(j * blk, (j + 1) * blk), slice(j * blk, rows)
            qq, gg = q[below, cols(h)], g[below, cols(h)]
            gk_part[here, cols(h)] = tn(dsc[h, below, here], qq) + scale * tn(
                din[h, below, here], qq
            )
            gv_part[here, cols(h)] = tn(probs[h, below, here], gg) + scale * tn(
                inner[h, below, here], gg
            )

    def backward_last(h):
        later = get_state(1, h)
        vv, kk = v[:, cols(h)], k[:, cols(h)]
        gk[:, cols(h)] = (gk_part[:, cols(h)] + nt(vv, later)).astype(BF16)
        gv[:, cols(h)] = (gv_part[:, cols(h)] + nn(kk, later)).astype(BF16)

    def store(i, src, dst):
        return pltpu.make_async_copy(src, dst, store_sem.at[i])

    def own_state():
        loads[0].wait()
        loads[1].wait()
        for h in range(heads):
            put_part(0, h, tn(k[:, cols(h)], v[:, cols(h)]))

    def own_grad():
        for h in range(heads):
            put_part(1, h, scale * tn(q[:, cols(h)], g[:, cols(h)]))

    def finish_sum():
        for half in range(2):
            acc = part_out[half, ahead[half]]
            for t in range(4):
                if streams[t][0] == half and rs_hops[t]:
                    got(rs_copy, t, rs_hops[t] - 1)
                    acc = acc + arrived[t, rs_hops[t] - 1].astype(F32)
            mixed[half] = acc.astype(BF16)

    results = ((gq, gq_out), (gk, gk_out), (gv, gv_out), (mixed, mixed_out))
    w_start()
    ag_forward(0)
    own_state()
    linear.start()
    loads[2].wait()
    w_spread()
    softmax_part(0)
    ag_forward(1)
    linear.middle()
    v_forward(0)
    softmax_part(1)
    linear.back()
    ag_forward(2)
    v_forward(1)
    ag_forward(3)
    linear.finish()
    for h in range(heads):
        attn_part(h)
    attn_exchange()
    v_forward(2)
    for load in loads[3:]:
        load.wait()
    grad_attn_part(0)
    w_finish()
    grad_attn_part(1)
    got(attn_copy, 1)
    project()
    rs_forward(0)
    g_collect()
    own_grad()
    trailing.start()
    backward_rows(0)
    backward_rows(1)
    store(0, gq, gq_out).start()
    rs_forward(1)
    trailing.middle()
    backward_columns(0)
    backward_columns(1)
    trailing.back()
    rs_forward(2)
    trailing.finish()
    for h in range(heads):
        backward_last(h)
    store(1, gk, gk_out).start()
    store(2, gv, gv_out).start()
    finish_sum()
    store(3, mixed, mixed_out).start()
    land()
    linear.drain()
    trailing.drain()
    for i, (src, dst) in enumerate(results):
        store(i, src, dst).wait()


def publish(*refs):
    sem = refs[-1]
    half = len(refs) // 2
    copies = [pltpu.make_async_copy(refs[i], refs[half + i], sem.at[i]) for i in range(half)]
    for copy in copies:
        copy.start()
    for copy in copies:
        copy.wait()


def on_device(sizes, length, query, key, value, block_mask, out_weight, cotangent):
    nz, group, groups, share = sizes
    rows, width = query.shape
    heads = width // DH
    dim = out_weight.shape[1]
    sub = rows // nz // 2
    span = nz // share
    hop = max(span // 2, 1)
    lines = group // 2
    cotangent = cotangent.reshape(2, sub, dim)
    out_weight = out_weight.reshape(2, lines, width // group, dim)
    piece = (heads * DH // group, DH)
    vmem, dma = pltpu.VMEM, pltpu.SemaphoreType.DMA
    any_space = pl.BlockSpec(memory_space=pl.ANY)
    square = (heads, rows, rows)
    rows_of = (2, span, sub)
    shapes = (
        jax.ShapeDtypeStruct((2, sub, dim), BF16),
        jax.ShapeDtypeStruct((rows, width), BF16),
        jax.ShapeDtypeStruct((rows, width), BF16),
        jax.ShapeDtypeStruct((rows, width), BF16),
    )
    outs = pl.pallas_call(
        functools.partial(kernel, sizes, length),
        out_shape=shapes,
        in_specs=[any_space] * 3 + [pl.BlockSpec(memory_space=pltpu.SMEM)] + [any_space] * 2,
        out_specs=(any_space,) * 4,
        scratch_shapes=[
            vmem((rows, width), BF16),
            vmem((rows, width), BF16),
            vmem((rows, width), BF16),
            vmem((share,) + out_weight.shape, BF16),
            vmem(rows_of + (dim,), BF16),
            vmem(square, BF16),
            vmem(square, BF16),
            vmem((heads, rows, DH), F32),
            vmem((heads, rows, DH), F32),
            vmem((nz, 2, sub, width), BF16),
            vmem((share,) + rows_of + (width,), BF16),
            vmem((share,) + rows_of + (width,), BF16),
            vmem(rows_of + (dim,), F32),
            vmem((share,) + rows_of + (width,), BF16),
            vmem((share,) + rows_of + (width,), BF16),
            vmem((nz, 2, sub, width), BF16),
            vmem((rows, width), BF16),
            vmem(square, BF16),
            vmem(square, BF16),
            vmem((rows, width), F32),
            vmem((rows, width), F32),
            vmem((rows, width), BF16),
            vmem((rows, width), BF16),
            vmem((rows, width), BF16),
            vmem((2, sub, dim), BF16),
            vmem((4, sub, dim), BF16),
            vmem((4, hop, sub, dim), BF16),
            vmem((2, group) + piece, F32),
            vmem((2, group) + piece, F32),
            vmem((2, group) + piece, F32),
            vmem((2, group) + piece, BF16),
            vmem((2,) + piece, F32),
            vmem((2, groups) + piece, F32),
            vmem((2, group) + piece, BF16),
            dma((6,)),
            dma((4,)),
        ]
        + [dma((4, hop))] * 4
        + [dma((2, group))] * 2
        + [dma((2, groups))] * 2
        + [dma((2, group))] * 2
        + [dma((share,))] * 2
        + [dma((lines,))] * 2
        + [dma((2, groups // 2))] * 2
        + [dma((2, groups // 2 + 1))] * 2
        + [dma((share,))] * 4,
        compiler_params=pltpu.CompilerParams(
            collective_id=0, has_side_effects=True, vmem_limit_bytes=56 << 20
        ),
        name="mixer",
    )(query, key, value, block_mask, out_weight, cotangent)
    outs = pl.pallas_call(
        publish,
        out_shape=shapes,
        in_specs=[pl.BlockSpec(memory_space=pltpu.VMEM)] * 4,
        out_specs=(any_space,) * 4,
        scratch_shapes=[dma((4,))],
        name="publish",
    )(*outs)
    return (outs[0].reshape(2 * sub, dim),) + tuple(outs[1:])


def solution(mesh):
    ctx = mesh.shape["ctx"]
    sizes = (mesh.shape["head"], GROUP, ctx // GROUP, SHARE)

    def step(query, key, value, block_mask, out_weight, cotangent):
        return on_device(
            sizes, query.shape[0] * ctx, query, key, value, block_mask, out_weight, cotangent
        )

    return jax.shard_map(
        step,
        mesh=mesh,
        in_specs=(
            P("ctx", "head"),
            P("ctx", "head"),
            P("ctx", "head"),
            P("ctx", None),
            P("head", None),
            P(("ctx", "head"), None),
        ),
        out_specs=(P(("ctx", "head"), None), P("ctx", "head"), P("ctx", "head"), P("ctx", "head")),
        check_vma=False,
    )
```
